128 devices in a mesh: strip: 128 (over z, x, y, core).
Axes of the slice: x: 4, y: 4, z: 4, core: 2. Of those that a mesh axis runs over, the one named last changes fastest.
Arguments:
- state: float32 [4096, 4096], P('strip'), may hold values from -6 to 6
- noise: float32 [4096, 4096], P('strip'), may hold values from -6 to 6
- step: float32 [1], replicated, may hold values from 0.3 to 0.7
- field_scale: float32 [1], replicated, may hold values from 0.6 to 1.2
- wave_scale: float32 [1], replicated, may hold values from 4 to 8
- source: float32 [2048, 2048], P('strip'), may hold values from -6 to 6
- obs_cells: int32 [8192], replicated, may hold values from 0 to 4194303
- obs_values: float32 [8192], replicated, may hold values from -3 to 3
Outputs:
- log_perm: float32 [2048, 2048], P('strip')
- pressure: float32 [2048, 2048], P('strip')
- loglik: float32 [], replicated
The draws below stay inside these ranges and needn't reach their ends.
Inputs may be any that keep to these rules, and one draw needn't show every extreme that they name: `obs_cells`: each entry is row * 2048 + column of an observed cell of the field grid.
All inputs are finite; a program needn't handle non-finite values.
Results may differ from the reference program's by a relative error of at most 0.00011.
Values sent between devices are 32-bit elements; how exact they have to be, the bound alone decides.
A program may use at most 64 MiB of HBM per device.

```python
import math
import jax
import jax.numpy as jnp

M = 4096
N = 2048
ITERS = 4
NOBS = 8192


def place_ends(values, own_key, smallest, high):
    dims = values.shape
    spot = [jax.random.randint(jax.random.fold_in(own_key, axis), (), 0, dims[axis]) for axis in range(len(dims))]
    values = values.at[tuple(spot)].set(smallest)
    longest = dims.index(max(dims))
    spot[longest] = (spot[longest] + 1) % dims[longest]
    return values.at[tuple(spot)].set(high)


def steps_of(stream_key, shape, pieces, smallest, high):
    def one(axis_at, shards_of):
        heights = jax.random.uniform(jax.random.fold_in(jax.random.fold_in(stream_key, 6), axis_at), (shards_of,), jnp.float32, smallest / len(pieces), high / len(pieces))
        return jnp.repeat(jnp.exp(heights), shape[axis_at] // shards_of).reshape((-1,) + (1,) * (len(shape) - axis_at - 1))

    gain = one(*pieces[0])
    for cut in pieces[1:]:
        gain = gain * one(*cut)
    return gain


def centred(stream_key, extent, scale, reach, cuts=(), kind=jnp.bfloat16):
    entries = jax.random.normal(stream_key, extent, jnp.float32) * scale
    if len(cuts) > 0:
        entries = steps_of(stream_key, extent, cuts, -0.22, 0.18) * entries
    return jnp.clip(entries, min=-reach, max=reach).astype(kind)


def setup_inputs(seed: int = 0) -> dict:
    key_of = jax.random.split(jax.random.key(seed), 9)
    state = centred(key_of[0], (M, M), 1.0, 6.0, ((0, 128),), jnp.float32)
    noise = centred(key_of[1], (M, M), 1.0, 6.0, ((0, 128),), jnp.float32)
    step = jnp.clip(jax.random.uniform(key_of[2], (1,), jnp.float32, 0.3, 0.7), 0.3, 0.7)
    field_scale = jnp.clip(jax.random.uniform(key_of[3], (1,), jnp.float32, 0.6, 1.2), 0.6, 1.2)
    wave_scale = jnp.clip(jax.random.uniform(key_of[4], (1,), jnp.float32, 4.0, 8.0), 4.0, 8.0)
    source = centred(key_of[5], (N, N), 1.0, 6.0, ((0, 128),), jnp.float32)
    obs_cells = place_ends(jax.random.randint(key_of[6], (NOBS,), 0, N * N), jax.random.fold_in(key_of[6], 1), 0, (N * N) - 1).astype(jnp.int32)
    obs_values = centred(key_of[7], (NOBS,), 0.5, 3.0, (), jnp.float32)
    return {"state": state, "noise": noise, "step": step, "field_scale": field_scale, "wave_scale": wave_scale, "source": source, "obs_cells": obs_cells, "obs_values": obs_values}


def amplitude(row_freq, col_freq, length, scale, wave):
    row_wave = jnp.minimum(row_freq, length - row_freq).astype(jnp.float32)
    col_wave = jnp.minimum(col_freq, length - col_freq).astype(jnp.float32)
    shape_term = 1.0 / (1.0 + (row_wave * row_wave + col_wave * col_wave) / (wave * wave))
    return scale * length / (wave * math.sqrt(math.pi)) * shape_term

def reference(state, noise, step, field_scale, wave_scale, source, obs_cells, obs_values):
    rate = step[0]
    mixed = jnp.sqrt(1.0 - rate * rate) * state + rate * noise
    row_freq = jnp.arange(M, dtype=jnp.int32)[:, None]
    col_freq = jnp.arange(M, dtype=jnp.int32)[None, :]
    scaled = amplitude(row_freq, col_freq, M, field_scale[0], wave_scale[0])
    spectrum = jnp.fft.fft2(mixed) * scaled
    log_perm = jnp.real(jnp.fft.ifft2(spectrum))[:N, :N]
    kappa = jnp.exp(log_perm)
    padded = jnp.pad(kappa, 1)
    north = 0.5 * (kappa + padded[:-2, 1:-1])
    south = 0.5 * (kappa + padded[2:, 1:-1])
    west = 0.5 * (kappa + padded[1:-1, :-2])
    east = 0.5 * (kappa + padded[1:-1, 2:])
    diagonal = north + south + west + east

    def operate(field):
        beside_all = jnp.pad(field, 1)
        return diagonal * field - north * beside_all[:-2, 1:-1] - south * beside_all[2:, 1:-1] - west * beside_all[1:-1, :-2] - east * beside_all[1:-1, 2:]
    pressure = jnp.zeros_like(source)
    residual = source
    precond = residual / diagonal
    direction = precond
    gamma = jnp.sum(residual * precond)
    for iteration in range(ITERS):
        image = operate(direction)
        alpha = gamma / jnp.sum(direction * image)
        pressure = pressure + alpha * direction
        residual = residual - alpha * image
        if iteration + 1 < ITERS:
            precond = residual / diagonal
            fresh = jnp.sum(residual * precond)
            direction = precond + fresh / gamma * direction
            gamma = fresh
    picked = pressure.reshape(-1)[obs_cells]
    differ = picked - obs_values
    loglik = -(2.0 / NOBS) * jnp.sum(differ * differ)
    return (log_perm, pressure, loglik)
```

```python
import functools
import math

import jax
import jax.numpy as jnp
import ml_dtypes
import numpy as np
from jax import lax
from jax.experimental import pallas as pl
from jax.experimental.pallas import tpu as pltpu
from jax.sharding import PartitionSpec as P

M = 4096
N = 2048
DEVICES = 128
ROWS = M // DEVICES
FIELD = N // DEVICES
KS = 80
AXIS = "strip"
MESH = pl.DeviceIdType.MESH
F32 = jnp.float32
BF16 = jnp.bfloat16


def halves(table):
    table = table.astype(np.float32)
    high = table.astype(ml_dtypes.bfloat16)
    low = (table - high.astype(np.float32)).astype(ml_dtypes.bfloat16)
    return np.stack([high, low])


def tables():
    b = np.arange(256)
    kl = np.arange(128)
    angle = 2 * np.pi * np.outer(kl, b) / 256
    top = np.zeros((16, 512))
    top[0, :256] = (-1.0) ** b
    row_forward = np.concatenate(
        [
            np.concatenate([np.cos(angle), np.sin(angle)], 1),
            np.concatenate([-np.sin(angle), np.cos(angle)], 1),
            top,
        ]
    )
    row_back = np.concatenate(
        [
            np.concatenate([np.cos(angle), np.sin(angle)], 1),
            np.concatenate([-np.sin(angle), np.cos(angle)], 1),
        ]
    )
    kv = np.arange(16)
    turn = 2 * np.pi * np.outer(kv, b) / M
    row_turn = np.stack([np.cos(turn), np.sin(turn)])
    ks = np.arange(KS)
    real = ks <= 64
    src = np.arange(DEVICES)
    angle = 2 * np.pi * np.outer(ks, src) / 128
    col_forward = np.concatenate([np.cos(angle), -np.sin(angle)]) * np.tile(real, 2)[:, None]
    weight = np.where((ks == 0) | (ks == 64), 1.0, 2.0) * real
    angle = angle.T[:64]
    col_back = np.concatenate([np.cos(angle) * weight, -np.sin(angle) * weight], 1)
    r = np.arange(32)
    lanes_in = [(v, q) for v in range(4) for q in range(32)]
    lanes_out = [(v, h * 16 + q) for h in range(2) for v in range(4) for q in range(16)]
    turn = 2 * np.pi * np.outer(ks, [q for _, q in lanes_in]) / M
    turn_back = 2 * np.pi * np.outer(ks, [q for _, q in lanes_out]) / M
    col_turn = np.stack([np.cos(turn), np.sin(turn), np.cos(turn_back), np.sin(turn_back)])
    vi, qi = np.array(lanes_in).T
    vo, qo = np.array(lanes_out).T
    same = vi[:, None] == vi[None, :]
    angle = 2 * np.pi * qi[:, None] * qi[None, :] / 32
    c, s = np.cos(angle) * same, np.sin(angle) * same
    mid_forward = np.block([[c, -s], [s, c]])
    same = vi[:, None] == vo[None, :]
    angle = 2 * np.pi * qi[:, None] * qo[None, :] / 32
    c, s = np.cos(angle) * same, np.sin(angle) * same
    mid_back = np.block([[c, s], [-s, c]])
    return (
        halves(row_forward),
        halves(row_back),
        row_turn.astype(np.float32),
        halves(col_forward),
        halves(col_back),
        col_turn.astype(np.float32),
        halves(mid_forward),
        halves(mid_back),
    )


def split(x):
    high = x.astype(BF16)
    return high, (x - high.astype(F32)).astype(BF16)


NN = (((1,), (0,)), ((), ()))
NT = (((1,), (1,)), ((), ()))


def product(left, right, form):
    dot = functools.partial(lax.dot_general, dimension_numbers=form, preferred_element_type=F32)
    (lh, ll), (rh, rl) = left, right
    return dot(lh, rh) + (dot(lh, rl) + dot(ll, rh))


def scaled(x, factor):
    if abs(factor) < 1e-12:
        return None
    if abs(factor - 1) < 1e-12:
        return x
    if abs(factor + 1) < 1e-12:
        return -x
    return x * F32(factor)


def plus(a, b):
    return b if a is None else a if b is None else a + b


def minus(a, b):
    if b is None:
        return a
    return -b if a is None else a - b


def turned(z, cos, sin):
    re, im = z
    out_re = scaled(re, cos) if re is not None else None
    out_im = scaled(re, sin) if re is not None else None
    if im is not None:
        out_re = minus(out_re, scaled(im, sin))
        out_im = plus(out_im, scaled(im, cos))
    return out_re, out_im


def added(a, b):
    return plus(a[0], b[0]), plus(a[1], b[1])


def less(a, b):
    return minus(a[0], b[0]), minus(a[1], b[1])


def real_dft(xs):
    count = len(xs)
    if count == 1:
        return [(xs[0], None)]
    even, odd = real_dft(xs[::2]), real_dft(xs[1::2])
    out = [None] * (count // 2 + 1)
    if count == 2:
        return [added(even[0], odd[0]), less(even[0], odd[0])]
    for k in range(count // 4 + 1):
        angle = -2 * math.pi * k / count
        t = turned(odd[k], math.cos(angle), math.sin(angle))
        out[k] = added(even[k], t)
        if k != count // 4:
            re, im = less(even[k], t)
            out[count // 2 - k] = (re, None if im is None else -im)
    return out


def back_dft(zs):
    count = len(zs)
    if count == 1:
        return list(zs)
    even, odd = back_dft(zs[::2]), back_dft(zs[1::2])
    out = [None] * count
    for k in range(count // 2):
        angle = 2 * math.pi * k / count
        t = turned(odd[k], math.cos(angle), math.sin(angle))
        out[k] = added(even[k], t)
        out[k + count // 2] = less(even[k], t)
    return out


def back_dft_real_first_half(zs):
    count = len(zs)
    even, odd = back_dft(zs[::2]), back_dft(zs[1::2])
    out = []
    for k in range(count // 2):
        angle = 2 * math.pi * k / count
        out.append(even[k][0] + turned(odd[k], math.cos(angle), math.sin(angle))[0])
    return out


def send_to_all(me, piece, landing, send_sem, recv_sem):
    @pl.loop(1, DEVICES)
    def _(i):
        other = lax.rem(me + i, DEVICES)
        pltpu.make_async_remote_copy(
            src_ref=piece(other),
            dst_ref=landing(me),
            send_sem=send_sem,
            recv_sem=recv_sem,
            device_id=(other,),
            device_id_type=MESH,
        ).start()


def wait_for_all(me, whole, send_sem, recv_sem):
    pltpu.make_async_remote_copy(
        src_ref=whole,
        dst_ref=whole,
        send_sem=send_sem,
        recv_sem=recv_sem,
        device_id=(lax.rem(me + 1, DEVICES),),
        device_id_type=MESH,
    ).wait()


def greet_all(me):
    barrier = pltpu.get_barrier_semaphore()

    @pl.loop(1, DEVICES)
    def _(i):
        pl.semaphore_signal(barrier, inc=1, device_id=(lax.rem(me + i, DEVICES),), device_id_type=MESH)


def meet_all():
    pl.semaphore_wait(pltpu.get_barrier_semaphore(), DEVICES - 1)


def rows_forward(rate, state, noise, row_turn, z_high, z_low, row_forward, out):
    keep = jnp.sqrt(1.0 - rate * rate)
    for g in range(ROWS // 16):
        rows = slice(16 * g, 16 * g + 16)
        for h in range(2):
            xs = []
            for a in range(16):
                cols = slice(256 * a + 128 * h, 256 * a + 128 * h + 128)
                xs.append(keep * state[rows, cols] + rate * noise[rows, cols])
            ys = real_dft(xs)
            for kv in range(16):
                re, im = ys[kv] if kv <= 8 else ys[16 - kv]
                cos = row_turn[0, kv : kv + 1, 128 * h : 128 * h + 128]
                sin = row_turn[1, kv : kv + 1, 128 * h : 128 * h + 128]
                if kv > 8:
                    im = -im
                if kv == 0:
                    zr, zi = re, jnp.zeros_like(re)
                elif im is None:
                    zr, zi = re * cos, -(re * sin)
                else:
                    zr, zi = re * cos + im * sin, im * cos - re * sin
                spot = slice(kv * ROWS + 16 * g, kv * ROWS + 16 * g + 16)
                for part, lane in ((zr, 128 * h), (zi, 256 + 128 * h)):
                    high, low = split(part)
                    z_high[spot, lane : lane + 128] = high
                    z_low[spot, lane : lane + 128] = low
    for pair in range(2):
        rows = slice(256 * pair, 256 * pair + 256)
        res = product((row_forward[0], row_forward[1]), (z_high[rows, :], z_low[rows, :]), NT)
        for i in range(2):
            t = 2 * pair + i
            lanes = slice(128 * i, 128 * i + 128)
            im = res[128:256, lanes]
            if t == 0:
                first = (lax.broadcasted_iota(jnp.int32, (128, 128), 0) == 0) & (
                    lax.broadcasted_iota(jnp.int32, (128, 128), 1) < ROWS
                )
                im = jnp.where(first, jnp.broadcast_to(res[256:257, lanes], (128, 128)), im)
            out[pl.ds(t, 128, stride=8), :] = res[:128, lanes]
            out[pl.ds(4 + t, 128, stride=8), :] = im


def amplitudes(me, sigma, wave, amp):
    ks = lax.broadcasted_iota(jnp.int32, (KS, 128), 0)
    lane = lax.broadcasted_iota(jnp.int32, (KS, 128), 1)
    k0 = ks + 128 * (lane % 32)
    q0 = jnp.minimum(k0, M - k0).astype(F32)
    base = q0 * q0 + wave * wave
    gain = sigma * wave * F32(2.0 / (math.sqrt(math.pi) * M))
    for v in range(4):
        k1 = 16 * me + 4 * v + lane // 32
        q1 = k1.astype(F32)
        value = gain / (base + q1 * q1)
        if v == 0:
            alone = k1 == 0
            value = jnp.where(alone, 0.5 * value, value)
            top = jnp.where(alone, 0.5 * gain / (base + F32(N) * F32(N)), value)
            amp[4] = top
        else:
            amp[4 + v] = value
        amp[v] = value


def columns(got, amp, col_forward, col_back, col_turn, mid_forward, mid_back, out):
    for u in range(4):
        pieces = jnp.concatenate([got[pl.ds(2 * u + i, 128, stride=8), :] for i in range(2)], axis=1)
        spec = product((col_forward[0], col_forward[1]), split(pieces), NN)
        parts = []
        for i in range(2):
            lanes = slice(128 * i, 128 * i + 128)
            re, im = spec[:KS, lanes], spec[KS:, lanes]
            cos, sin = col_turn[0], col_turn[1]
            parts.append(jnp.concatenate([re * cos + im * sin, im * cos - re * sin], axis=1))
        full = product(split(jnp.concatenate(parts, axis=0)), (mid_forward[0], mid_forward[1]), NN)
        factor = jnp.concatenate([amp[2 * u], amp[2 * u + 1]], axis=0)
        full = full * jnp.concatenate([factor, factor], axis=1)
        back = product(split(full), (mid_back[0], mid_back[1]), NN)
        sides = []
        for i in range(2):
            rows = slice(KS * i, KS * i + KS)
            re, im = back[rows, :128], back[rows, 128:]
            cos, sin = col_turn[2], col_turn[3]
            sides.append(jnp.concatenate([re * cos - im * sin, im * cos + re * sin], axis=0))
        field = product((col_back[0], col_back[1]), split(jnp.concatenate(sides, axis=1)), NN)
        left, right = field[:, :128], field[:, 128:]
        low = lax.broadcasted_iota(jnp.int32, (64, 128), 1) < 64
        out[pl.ds(u, 64, stride=8), :] = jnp.where(low, left, pltpu.roll(right, 64, 1))
        out[pl.ds(4 + u, 64, stride=8), :] = jnp.where(low, pltpu.roll(left, 64, 1), right)


def rows_back(got, row_back, row_turn, put):
    blocks = [got[pl.ds(u, 128, stride=4), :].T for u in range(4)]
    re = jnp.concatenate(blocks[:2], axis=0)
    im = jnp.concatenate(blocks[2:], axis=0)
    corner = (lax.broadcasted_iota(jnp.int32, (256, 128), 0) < FIELD) & (
        lax.broadcasted_iota(jnp.int32, (256, 128), 1) == 0
    )
    top = jnp.broadcast_to(im[:FIELD, :1], (FIELD, 128))
    sign = (1 - 2 * (lax.broadcasted_iota(jnp.int32, (FIELD, 128), 1) % 2)).astype(F32)
    top = top * sign
    im = jnp.where(corner, 0.0, im)
    q = product(split(jnp.concatenate([re, im], axis=1)), (row_back[0], row_back[1]), NN)
    for h in range(2):
        zs = []
        for kv in range(16):
            rows = slice(FIELD * kv, FIELD * kv + FIELD)
            zr, zi = q[rows, 128 * h : 128 * h + 128], q[rows, 256 + 128 * h : 384 + 128 * h]
            cos = row_turn[0, kv : kv + 1, 128 * h : 128 * h + 128]
            sin = row_turn[1, kv : kv + 1, 128 * h : 128 * h + 128]
            zs.append((zr, zi) if kv == 0 else (zr * cos - zi * sin, zi * cos + zr * sin))
        for a, value in enumerate(back_dft_real_first_half(zs)):
            put(256 * a + 128 * h, value + top)


def transform_kernel(
    step, sigma, wave, state, noise, row_forward, row_back, row_turn, col_forward, col_back, col_turn,
    mid_forward, mid_back, log_perm, z_high, z_low, sent1, got1, amp, sent2, got2, sems,
):
    me = lax.axis_index(AXIS)
    greet_all(me)
    rows_forward(step[0], state, noise, row_turn, z_high, z_low, row_forward, sent1)
    meet_all()
    send_to_all(me, lambda d: sent1.at[pl.ds(8 * d, 8), :], lambda s: got1.at[pl.ds(8 * s, 8), :], sems.at[0], sems.at[1])
    own = pl.ds(pl.multiple_of(8 * me, 8), 8)
    got1[own, :] = sent1[own, :]
    amplitudes(me, sigma[0], wave[0], amp)
    wait_for_all(me, got1.at[pl.ds(0, 8 * (DEVICES - 1)), :], sems.at[0], sems.at[1])
    columns(got1, amp, col_forward, col_back, col_turn, mid_forward, mid_back, sent2)
    send_to_all(me, lambda d: sent2.at[pl.ds(4 * d, 4), :], lambda s: got2.at[pl.ds(4 * s, 4), :], sems.at[2], sems.at[3])
    own = pl.ds(pl.multiple_of(4 * me, 4), 4)
    got2[own, :] = sent2[own, :]
    wait_for_all(me, got2.at[pl.ds(0, 4 * (DEVICES - 1)), :], sems.at[2], sems.at[3])

    def put(at, value):
        log_perm[:, at : at + 128] = value

    rows_back(got2, row_back, row_turn, put)


def log_permeability(step, sigma, wave, state, noise):
    vmem = pl.BlockSpec(memory_space=pltpu.VMEM)
    smem = pl.BlockSpec(memory_space=pltpu.SMEM)
    return pl.pallas_call(
        transform_kernel,
        out_shape=jax.ShapeDtypeStruct((FIELD, N), F32),
        in_specs=[smem] * 3 + [vmem] * 10,
        out_specs=vmem,
        scratch_shapes=[
            pltpu.VMEM((512, 512), BF16),
            pltpu.VMEM((512, 512), BF16),
            pltpu.VMEM((1024, 128), F32),
            pltpu.VMEM((1024, 128), F32),
            pltpu.VMEM((8, KS, 128), F32),
            pltpu.VMEM((512, 128), F32),
            pltpu.VMEM((512, 128), F32),
            pltpu.SemaphoreType.DMA((4,)),
        ],
        compiler_params=pltpu.CompilerParams(collective_id=0, has_side_effects=True, vmem_limit_bytes=60 * 2**20),
    )(step, sigma, wave, state, noise, *[jnp.asarray(t) for t in tables()])


def padded(block):
    forward = [(i, i + 1) for i in range(DEVICES - 1)]
    backward = [(i + 1, i) for i in range(DEVICES - 1)]
    low = lax.ppermute(block[-1:], AXIS, forward)
    high = lax.ppermute(block[:1], AXIS, backward)
    return jnp.concatenate([low, block, high], axis=0)


def body(state, noise, step, field_scale, wave_scale, source, obs_cells, obs_values):
    position = lax.axis_index(AXIS)
    log_perm = log_permeability(step, field_scale, wave_scale, state, noise)
    kappa = jnp.exp(log_perm)
    rimmed = padded(kappa)
    sided = jnp.pad(kappa, ((0, 0), (1, 1)))
    north = 0.5 * (kappa + rimmed[:-2])
    south = 0.5 * (kappa + rimmed[2:])
    west = 0.5 * (kappa + sided[:, :-2])
    east = 0.5 * (kappa + sided[:, 2:])
    diagonal = north + south + west + east
    pressure = jnp.zeros_like(source)
    residual = source
    direction = jnp.zeros_like(source)
    along = jnp.zeros_like(source)
    gamma_prior = jnp.float32(1.0)
    alpha_prior = jnp.float32(1.0)
    for iteration in range(4):
        precond = residual / diagonal
        beside_all = padded(precond)
        beside = jnp.pad(precond, ((0, 0), (1, 1)))
        image = (
            diagonal * precond
            - north * beside_all[:-2]
            - south * beside_all[2:]
            - west * beside[:, :-2]
            - east * beside[:, 2:]
        )
        gamma, delta = lax.psum(jnp.stack([jnp.sum(residual * precond), jnp.sum(precond * image)]), AXIS)
        if iteration == 0:
            alpha = gamma / delta
            direction = precond
            along = image
        else:
            ratio = gamma / gamma_prior
            alpha = gamma / (delta - ratio * gamma / alpha_prior)
            direction = precond + ratio * direction
            along = image + ratio * along
        pressure = pressure + alpha * direction
        residual = residual - alpha * along
        gamma_prior = gamma
        alpha_prior = alpha
    columns_here = pressure.shape[1]
    cell_row = obs_cells // columns_here
    cell_col = obs_cells % columns_here
    local_row = cell_row - position * FIELD
    inside = (local_row >= 0) & (local_row < FIELD)
    picked = pressure[jnp.clip(local_row, 0, FIELD - 1), cell_col]
    differ = jnp.where(inside, picked - obs_values, 0.0)
    total = lax.psum(jnp.sum(differ * differ), AXIS)
    loglik = -(2.0 / obs_cells.shape[0]) * total
    return (log_perm, pressure, loglik)


def solution(mesh):
    in_specs = (P(AXIS, None), P(AXIS, None), P(), P(), P(), P(AXIS, None), P(), P())
    out_specs = (P(AXIS, None), P(AXIS, None), P())
    return jax.shard_map(body, mesh=mesh, in_specs=in_specs, out_specs=out_specs, check_vma=False)
```

```python
import functools
import math

import jax
import jax.numpy as jnp
import ml_dtypes
import numpy as np
from jax import lax
from jax.experimental import pallas as pl
from jax.experimental.pallas import tpu as pltpu
from jax.sharding import PartitionSpec as P

M = 4096
N = 2048
DEVICES = 128
ROWS = M // DEVICES
FIELD = N // DEVICES
KS = 80
AXIS = "strip"
MESH = pl.DeviceIdType.MESH
F32 = jnp.float32
BF16 = jnp.bfloat16


def halves(table):
    table = table.astype(np.float32)
    high = table.astype(ml_dtypes.bfloat16)
    low = (table - high.astype(np.float32)).astype(ml_dtypes.bfloat16)
    return np.stack([high, low])


def tables():
    b = np.arange(256)
    kl = np.arange(128)
    angle = 2 * np.pi * np.outer(kl, b) / 256
    top = np.zeros((16, 512))
    top[0, :256] = (-1.0) ** b
    row_forward = np.concatenate(
        [
            np.concatenate([np.cos(angle), np.sin(angle)], 1),
            np.concatenate([-np.sin(angle), np.cos(angle)], 1),
            top,
        ]
    )
    row_back = np.concatenate(
        [
            np.concatenate([np.cos(angle), np.sin(angle)], 1),
            np.concatenate([-np.sin(angle), np.cos(angle)], 1),
        ]
    )
    kv = np.arange(16)
    turn = 2 * np.pi * np.outer(kv, b) / M
    row_turn = np.stack([np.cos(turn), np.sin(turn)])
    ks = np.arange(KS)
    real = ks <= 64
    src = np.arange(DEVICES)
    angle = 2 * np.pi * np.outer(ks, src) / 128
    col_forward = np.concatenate([np.cos(angle), -np.sin(angle)]) * np.tile(real, 2)[:, None]
    weight = np.where((ks == 0) | (ks == 64), 1.0, 2.0) * real
    angle = angle.T[:64]
    col_back = np.concatenate([np.cos(angle) * weight, -np.sin(angle) * weight], 1)
    r = np.arange(32)
    lanes_in = [(v, q) for v in range(4) for q in range(32)]
    lanes_out = [(v, h * 16 + q) for h in range(2) for v in range(4) for q in range(16)]
    turn = 2 * np.pi * np.outer(ks, [q for _, q in lanes_in]) / M
    turn_back = 2 * np.pi * np.outer(ks, [q for _, q in lanes_out]) / M
    col_turn = np.stack([np.cos(turn), np.sin(turn), np.cos(turn_back), np.sin(turn_back)])
    vi, qi = np.array(lanes_in).T
    vo, qo = np.array(lanes_out).T
    same = vi[:, None] == vi[None, :]
    angle = 2 * np.pi * qi[:, None] * qi[None, :] / 32
    c, s = np.cos(angle) * same, np.sin(angle) * same
    mid_forward = np.block([[c, -s], [s, c]])
    same = vi[:, None] == vo[None, :]
    angle = 2 * np.pi * qi[:, None] * qo[None, :] / 32
    c, s = np.cos(angle) * same, np.sin(angle) * same
    mid_back = np.block([[c, s], [-s, c]])
    return (
        halves(row_forward),
        halves(row_back),
        row_turn.astype(np.float32),
        halves(col_forward),
        halves(col_back),
        col_turn.astype(np.float32),
        halves(mid_forward),
        halves(mid_back),
    )


def split(x):
    high = x.astype(BF16)
    return high, (x - high.astype(F32)).astype(BF16)


NN = (((1,), (0,)), ((), ()))
NT = (((1,), (1,)), ((), ()))


def product(left, right, form):
    dot = functools.partial(lax.dot_general, dimension_numbers=form, preferred_element_type=F32)
    (lh, ll), (rh, rl) = left, right
    return dot(lh, rh) + (dot(lh, rl) + dot(ll, rh))


def scaled(x, factor):
    if abs(factor) < 1e-12:
        return None
    if abs(factor - 1) < 1e-12:
        return x
    if abs(factor + 1) < 1e-12:
        return -x
    return x * F32(factor)


def plus(a, b):
    return b if a is None else a if b is None else a + b


def minus(a, b):
    if b is None:
        return a
    return -b if a is None else a - b


def turned(z, cos, sin):
    re, im = z
    out_re = scaled(re, cos) if re is not None else None
    out_im = scaled(re, sin) if re is not None else None
    if im is not None:
        out_re = minus(out_re, scaled(im, sin))
        out_im = plus(out_im, scaled(im, cos))
    return out_re, out_im


def added(a, b):
    return plus(a[0], b[0]), plus(a[1], b[1])


def less(a, b):
    return minus(a[0], b[0]), minus(a[1], b[1])


def real_dft(xs):
    count = len(xs)
    if count == 1:
        return [(xs[0], None)]
    even, odd = real_dft(xs[::2]), real_dft(xs[1::2])
    out = [None] * (count // 2 + 1)
    if count == 2:
        return [added(even[0], odd[0]), less(even[0], odd[0])]
    for k in range(count // 4 + 1):
        angle = -2 * math.pi * k / count
        t = turned(odd[k], math.cos(angle), math.sin(angle))
        out[k] = added(even[k], t)
        if k != count // 4:
            re, im = less(even[k], t)
            out[count // 2 - k] = (re, None if im is None else -im)
    return out


def back_dft(zs):
    count = len(zs)
    if count == 1:
        return list(zs)
    even, odd = back_dft(zs[::2]), back_dft(zs[1::2])
    out = [None] * count
    for k in range(count // 2):
        angle = 2 * math.pi * k / count
        t = turned(odd[k], math.cos(angle), math.sin(angle))
        out[k] = added(even[k], t)
        out[k + count // 2] = less(even[k], t)
    return out


def back_dft_real_first_half(zs):
    count = len(zs)
    even, odd = back_dft(zs[::2]), back_dft(zs[1::2])
    out = []
    for k in range(count // 2):
        angle = 2 * math.pi * k / count
        out.append(even[k][0] + turned(odd[k], math.cos(angle), math.sin(angle))[0])
    return out


def send_to_all(me, piece, landing, send_sem, recv_sem):
    @pl.loop(1, DEVICES)
    def _(i):
        other = lax.rem(me + i, DEVICES)
        pltpu.make_async_remote_copy(
            src_ref=piece(other),
            dst_ref=landing(me),
            send_sem=send_sem,
            recv_sem=recv_sem,
            device_id=(other,),
            device_id_type=MESH,
        ).start()


def wait_for_all(me, whole, send_sem, recv_sem):
    pltpu.make_async_remote_copy(
        src_ref=whole,
        dst_ref=whole,
        send_sem=send_sem,
        recv_sem=recv_sem,
        device_id=(lax.rem(me + 1, DEVICES),),
        device_id_type=MESH,
    ).wait()


def greet_all(me):
    barrier = pltpu.get_barrier_semaphore()

    @pl.loop(1, DEVICES)
    def _(i):
        pl.semaphore_signal(barrier, inc=1, device_id=(lax.rem(me + i, DEVICES),), device_id_type=MESH)


def meet_all():
    pl.semaphore_wait(pltpu.get_barrier_semaphore(), DEVICES - 1)


def rows_forward(rate, state, noise, row_turn, z_high, z_low, row_forward, out):
    keep = jnp.sqrt(1.0 - rate * rate)
    for g in range(ROWS // 16):
        rows = slice(16 * g, 16 * g + 16)
        for h in range(2):
            xs = []
            for a in range(16):
                cols = slice(256 * a + 128 * h, 256 * a + 128 * h + 128)
                xs.append(keep * state[rows, cols] + rate * noise[rows, cols])
            ys = real_dft(xs)
            for kv in range(16):
                re, im = ys[kv] if kv <= 8 else ys[16 - kv]
                cos = row_turn[0, kv : kv + 1, 128 * h : 128 * h + 128]
                sin = row_turn[1, kv : kv + 1, 128 * h : 128 * h + 128]
                if kv > 8:
                    im = -im
                if kv == 0:
                    zr, zi = re, jnp.zeros_like(re)
                elif im is None:
                    zr, zi = re * cos, -(re * sin)
                else:
                    zr, zi = re * cos + im * sin, im * cos - re * sin
                spot = slice(kv * ROWS + 16 * g, kv * ROWS + 16 * g + 16)
                for part, lane in ((zr, 128 * h), (zi, 256 + 128 * h)):
                    high, low = split(part)
                    z_high[spot, lane : lane + 128] = high
                    z_low[spot, lane : lane + 128] = low
    for pair in range(2):
        rows = slice(256 * pair, 256 * pair + 256)
        res = product((row_forward[0], row_forward[1]), (z_high[rows, :], z_low[rows, :]), NT)
        for i in range(2):
            t = 2 * pair + i
            lanes = slice(128 * i, 128 * i + 128)
            im = res[128:256, lanes]
            if t == 0:
                first = (lax.broadcasted_iota(jnp.int32, (128, 128), 0) == 0) & (
                    lax.broadcasted_iota(jnp.int32, (128, 128), 1) < ROWS
                )
                im = jnp.where(first, jnp.broadcast_to(res[256:257, lanes], (128, 128)), im)
            out[pl.ds(t, 128, stride=8), :] = res[:128, lanes]
            out[pl.ds(4 + t, 128, stride=8), :] = im


def amplitudes(me, sigma, wave, amp):
    ks = lax.broadcasted_iota(jnp.int32, (KS, 128), 0)
    lane = lax.broadcasted_iota(jnp.int32, (KS, 128), 1)
    k0 = ks + 128 * (lane % 32)
    q0 = jnp.minimum(k0, M - k0).astype(F32)
    base = q0 * q0 + wave * wave
    gain = sigma * wave * F32(2.0 / (math.sqrt(math.pi) * M))
    for v in range(4):
        k1 = 16 * me + 4 * v + lane // 32
        q1 = k1.astype(F32)
        value = gain / (base + q1 * q1)
        if v == 0:
            alone = k1 == 0
            value = jnp.where(alone, 0.5 * value, value)
            top = jnp.where(alone, 0.5 * gain / (base + F32(N) * F32(N)), value)
            amp[4] = top
        else:
            amp[4 + v] = value
        amp[v] = value


def columns(got, amp, col_forward, col_back, col_turn, mid_forward, mid_back, out):
    for u in range(4):
        pieces = jnp.concatenate([got[pl.ds(2 * u + i, 128, stride=8), :] for i in range(2)], axis=1)
        spec = product((col_forward[0], col_forward[1]), split(pieces), NN)
        parts = []
        for i in range(2):
            lanes = slice(128 * i, 128 * i + 128)
            re, im = spec[:KS, lanes], spec[KS:, lanes]
            cos, sin = col_turn[0], col_turn[1]
            parts.append(jnp.concatenate([re * cos + im * sin, im * cos - re * sin], axis=1))
        full = product(split(jnp.concatenate(parts, axis=0)), (mid_forward[0], mid_forward[1]), NN)
        factor = jnp.concatenate([amp[2 * u], amp[2 * u + 1]], axis=0)
        full = full * jnp.concatenate([factor, factor], axis=1)
        back = product(split(full), (mid_back[0], mid_back[1]), NN)
        sides = []
        for i in range(2):
            rows = slice(KS * i, KS * i + KS)
            re, im = back[rows, :128], back[rows, 128:]
            cos, sin = col_turn[2], col_turn[3]
            sides.append(jnp.concatenate([re * cos - im * sin, im * cos + re * sin], axis=0))
        field = product((col_back[0], col_back[1]), split(jnp.concatenate(sides, axis=1)), NN)
        left, right = field[:, :128], field[:, 128:]
        low = lax.broadcasted_iota(jnp.int32, (64, 128), 1) < 64
        out[pl.ds(u, 64, stride=8), :] = jnp.where(low, left, pltpu.roll(right, 64, 1))
        out[pl.ds(4 + u, 64, stride=8), :] = jnp.where(low, pltpu.roll(left, 64, 1), right)


def rows_back(got, row_back, row_turn, put):
    blocks = [got[pl.ds(u, 128, stride=4), :].T for u in range(4)]
    re = jnp.concatenate(blocks[:2], axis=0)
    im = jnp.concatenate(blocks[2:], axis=0)
    corner = (lax.broadcasted_iota(jnp.int32, (256, 128), 0) < FIELD) & (
        lax.broadcasted_iota(jnp.int32, (256, 128), 1) == 0
    )
    top = jnp.broadcast_to(im[:FIELD, :1], (FIELD, 128))
    sign = (1 - 2 * (lax.broadcasted_iota(jnp.int32, (FIELD, 128), 1) % 2)).astype(F32)
    top = top * sign
    im = jnp.where(corner, 0.0, im)
    q = product(split(jnp.concatenate([re, im], axis=1)), (row_back[0], row_back[1]), NN)
    for h in range(2):
        zs = []
        for kv in range(16):
            rows = slice(FIELD * kv, FIELD * kv + FIELD)
            zr, zi = q[rows, 128 * h : 128 * h + 128], q[rows, 256 + 128 * h : 384 + 128 * h]
            cos = row_turn[0, kv : kv + 1, 128 * h : 128 * h + 128]
            sin = row_turn[1, kv : kv + 1, 128 * h : 128 * h + 128]
            zs.append((zr, zi) if kv == 0 else (zr * cos - zi * sin, zi * cos + zr * sin))
        for a, value in enumerate(back_dft_real_first_half(zs)):
            put(256 * a + 128 * h, value + top)


def gather_observations(me, cells, values, counts, means, hot, parts):
    counts[...] = jnp.zeros_like(counts)

    @pl.loop(0, 8)
    def _(c):
        for i in range(8):
            cell = cells[pl.ds(8 * c + i, 1), :]
            value = values[pl.ds(8 * c + i, 1), :]
            row = cell // N - FIELD * me
            col = cell % N
            inside = (row >= 0) & (row < FIELD)
            spot = jnp.where(inside, (row // 8) * 128 + (col // 128) * 8 + row % 8, -1)
            lane = jnp.where(inside, col % 128, -1)
            lanes = slice(128 * i, 128 * i + 128)
            here = lax.broadcasted_iota(jnp.int32, (256, 128), 0) == spot
            hot[c, :, lanes] = jnp.where(here, 1.0, 0.0).astype(BF16)
            there = lax.broadcasted_iota(jnp.int32, (128, 128), 0) == lane
            high = value.astype(BF16).astype(F32)
            middle = (value - high).astype(BF16).astype(F32)
            low = value - high - middle
            for j, piece in enumerate((jnp.ones_like(value), high, middle, low)):
                parts[128 * j : 128 * j + 128, lanes] = jnp.where(there, piece, 0.0).astype(BF16)
        counts[...] += lax.dot_general(hot[c], parts[...], NT, preferred_element_type=F32)

    number = counts[:, :128]
    total = counts[:, 128:256] + counts[:, 256:384] + counts[:, 384:]
    means[...] = total / jnp.maximum(number, 1.0)


def spread_observations(me, cells, values, means, hot, pieces, spread):
    turned_means = jnp.concatenate([means[:128, :].T, means[128:, :].T], axis=1)
    high = turned_means.astype(BF16)
    rest = turned_means - high.astype(F32)
    middle = rest.astype(BF16)
    pieces[:128, :] = high
    pieces[128:256, :] = middle
    pieces[256:, :] = (rest - middle.astype(F32)).astype(BF16)
    spread[...] = jnp.zeros_like(spread)

    @pl.loop(0, 8)
    def _(c):
        picked = jnp.dot(pieces[...], hot[c], preferred_element_type=F32)
        total = jnp.zeros((8, 128), F32)
        for i in range(8):
            cell = cells[pl.ds(8 * c + i, 1), :]
            value = values[pl.ds(8 * c + i, 1), :]
            row = cell // N - FIELD * me
            inside = (row >= 0) & (row < FIELD)
            lane = jnp.where(inside, cell % 128, -1)
            lanes = slice(128 * i, 128 * i + 128)
            mean = picked[:128, lanes] + (picked[128:256, lanes] + picked[256:, lanes])
            there = lax.broadcasted_iota(jnp.int32, (128, 128), 0) == lane
            off = jnp.where(there, value - mean, 0.0)
            off = off * off
            for k in range(16):
                total = total + off[8 * k : 8 * k + 8]
        spread[...] += total


def exchange_edges(me, own_low, own_high, ext, sems):
    up, down = lax.rem(me + 1, DEVICES), lax.rem(me + DEVICES - 1, DEVICES)
    return [
        pltpu.make_async_remote_copy(
            src_ref=own_low, dst_ref=ext.at[pl.ds(24, 8), :], send_sem=sems.at[0], recv_sem=sems.at[1],
            device_id=(down,), device_id_type=MESH,
        ),
        pltpu.make_async_remote_copy(
            src_ref=own_high, dst_ref=ext.at[pl.ds(0, 8), :], send_sem=sems.at[2], recv_sem=sems.at[3],
            device_id=(up,), device_id_type=MESH,
        ),
    ]


TILES = N // 128
OWN = slice(8, 24)


def tile(j):
    return slice(128 * j, 128 * j + 128)


def neighbours(load):
    lane = lax.broadcasted_iota(jnp.int32, (32, 128), 1)
    values = [load(0), load(1)]
    rights = [pltpu.roll(v, 1, 1) for v in values]
    lefts = [pltpu.roll(v, 127, 1) for v in values]
    before = jnp.zeros_like(rights[0])
    for j in range(TILES):
        if j == TILES - 1:
            after = jnp.zeros_like(before)
        else:
            after = lefts[1]
        west = jnp.where(lane == 0, before, rights[0])
        east = jnp.where(lane == 127, after, lefts[0])
        north = pltpu.roll(values[0], 1, 0)
        south = pltpu.roll(values[0], 31, 0)
        yield j, values[0], north, south, west, east
        before = rights[0]
        if j + 1 < TILES:
            values = values[1:]
            rights = rights[1:]
            lefts = lefts[1:]
            if j + 2 < TILES:
                values.append(load(j + 2))
                rights.append(pltpu.roll(values[1], 1, 1))
                lefts.append(pltpu.roll(values[1], 127, 1))


def krylov(me, lx, sx, kappa, coefs, diag, v0, z0, z1, z2):
    row = lax.broadcasted_iota(jnp.int32, (32, 128), 0)
    lane = lax.broadcasted_iota(jnp.int32, (32, 128), 1)
    valid = ((row >= 8) | (me > 0)) & ((row < 24) | (me < DEVICES - 1))
    for j in range(TILES):
        kappa[:, tile(j)] = jnp.where(valid, jnp.exp(lx[:, tile(j)]), 0.0)
    sums = [jnp.zeros((16, 128), F32) for _ in range(8)]
    for j, k, kn, ks, kw, ke in neighbours(lambda j: kappa[:, tile(j)]):
        north, south, west, east = 0.5 * (k + kn), 0.5 * (k + ks), 0.5 * (k + kw), 0.5 * (k + ke)
        d = north + south + west + east
        inverse = jnp.where(valid, 1.0 / d, 0.0)
        coefs[0, :, tile(j)] = north * inverse
        coefs[1, :, tile(j)] = south * inverse
        coefs[2, :, tile(j)] = west * inverse
        coefs[3, :, tile(j)] = east * inverse
        source = sx[:, tile(j)]
        first = source * inverse
        diag[:, tile(j)] = d[OWN]
        v0[:, tile(j)] = first
        sums[0] = sums[0] + source[OWN] * first[OWN]

    def beside(values):
        for j, v, vn, vs, vw, ve in neighbours(lambda j: values[:, tile(j)]):
            yield j, v, (coefs[0, :, tile(j)] * vn + coefs[1, :, tile(j)] * vs) + (
                coefs[2, :, tile(j)] * vw + coefs[3, :, tile(j)] * ve
            )

    for j, v, s in beside(v0):
        z = v - s
        z0[:, tile(j)] = z
        own = z[OWN]
        sums[1] = sums[1] + sx[OWN, tile(j)] * own
        sums[2] = sums[2] + diag[:, tile(j)] * own * own
    for j, v, s in beside(z0):
        z = -s
        z1[:, tile(j)] = z
        own = diag[:, tile(j)] * z[OWN]
        sums[3] = sums[3] + own * v[OWN]
        sums[4] = sums[4] + own * z[OWN]
    for j, v, s in beside(z1):
        z = -2.0 * s - z0[:, tile(j)]
        z2[:, tile(j)] = z
        own = diag[:, tile(j)] * z[OWN]
        sums[5] = sums[5] + own * v[OWN]
        sums[6] = sums[6] + own * z[OWN]
    for j, v, s in beside(z2):
        z = -2.0 * s[OWN] - z1[OWN, tile(j)]
        sums[7] = sums[7] + diag[:, tile(j)] * v[OWN] * z
    return sums


def lane_totals(sums):
    rows = jnp.concatenate([jnp.sum(s, axis=0, keepdims=True) for s in sums], axis=0)
    totals = jnp.broadcast_to(jnp.sum(rows, axis=1, keepdims=True), (8, 128))
    at = lax.broadcasted_iota(jnp.int32, (8, 128), 0) == lax.broadcasted_iota(jnp.int32, (8, 128), 1)
    return jnp.sum(jnp.where(at, totals, 0.0), axis=0, keepdims=True)


def share(me, row, mine, all_rows, sems):
    mine[0:1, :] = row
    all_rows[pl.ds(me, 1), :] = row
    send_to_all(me, lambda d: mine.at[pl.ds(0, 1), :], lambda s: all_rows.at[pl.ds(s, 1), :], sems.at[0], sems.at[1])
    wait_for_all(me, all_rows.at[pl.ds(0, DEVICES - 1), :], sems.at[0], sems.at[1])
    return jnp.sum(all_rows[...], axis=0, keepdims=True)


def weights(row):
    take = [jnp.broadcast_to(row[:, i : i + 1], (16, 128)) for i in range(8)]
    g0, e0, m0, m1, q11, q12, q22, q23 = take
    m2 = 2.0 * q11 - m0
    m3 = 2.0 * q12 - m1
    m4 = 2.0 * q22 - m0
    m5 = 2.0 * q23 - m1
    m = [m0, m1, m2, m3, m4, m5]

    def inner(i, j):
        return 0.5 * (m[i + j] + m[abs(i - j)])

    def energy(i, j):
        return inner(i, j) + 0.5 * (inner(i, j + 1) + inner(i, abs(j - 1)))

    gram = [[None] * 4 for _ in range(4)]
    gram[0][0] = e0
    for j in range(3):
        gram[j + 1][0] = inner(0, j)
        for i in range(j + 1):
            gram[j + 1][i + 1] = energy(i, j)
    right = [g0, e0, m0 - e0, 2.0 * (m1 - (m0 - e0)) - e0]
    factors = [[None] * 4 for _ in range(4)]
    inverse = []
    whole = [gram[i][i] for i in range(4)]
    for k in range(4):
        pivot = gram[k][k]
        inverse.append(jnp.where(pivot > 1e-6 * whole[k], 1.0 / pivot, 0.0))
        for i in range(k + 1, 4):
            factors[i][k] = gram[i][k] * inverse[k]
        for i in range(k + 1, 4):
            for j in range(k + 1, i + 1):
                gram[i][j] = gram[i][j] - factors[i][k] * gram[j][k]
            right[i] = right[i] - factors[i][k] * right[k]
    out = [right[k] * inverse[k] for k in range(4)]
    for k in (2, 1, 0):
        for i in range(k + 1, 4):
            out[k] = out[k] - factors[i][k] * out[i]
    return out


def kernel(
    step, sigma, wave, state, noise, source, cells, values,
    row_forward, row_back, row_turn, col_forward, col_back, col_turn, mid_forward, mid_back,
    log_perm, pressure, loglik,
    z_high, z_low, sent1, got1, amp, sent2, got2,
    counts, means, hot, parts, pieces, spread,
    lx, sx, kappa, coefs, diag, v0, z0, z1, z2, mine, everyone, sems,
):
    me = lax.axis_index(AXIS)
    greet_all(me)
    rows_forward(step[0], state, noise, row_turn, z_high, z_low, row_forward, sent1)
    meet_all()
    send_to_all(me, lambda d: sent1.at[pl.ds(8 * d, 8), :], lambda s: got1.at[pl.ds(8 * s, 8), :], sems.at[0], sems.at[1])
    source_edges = exchange_edges(me, source.at[pl.ds(0, 8), :], source.at[pl.ds(8, 8), :], sx, sems.at[pl.ds(4, 4)])
    for copy in source_edges:
        copy.start()
    own = pl.ds(pl.multiple_of(8 * me, 8), 8)
    got1[own, :] = sent1[own, :]
    sx[OWN, :] = source[...]
    amplitudes(me, sigma[0], wave[0], amp)
    gather_observations(me, cells, values, counts, means, hot, parts)
    wait_for_all(me, got1.at[pl.ds(0, 8 * (DEVICES - 1)), :], sems.at[0], sems.at[1])
    columns(got1, amp, col_forward, col_back, col_turn, mid_forward, mid_back, sent2)
    send_to_all(me, lambda d: sent2.at[pl.ds(4 * d, 4), :], lambda s: got2.at[pl.ds(4 * s, 4), :], sems.at[2], sems.at[3])
    own = pl.ds(pl.multiple_of(4 * me, 4), 4)
    got2[own, :] = sent2[own, :]
    spread_observations(me, cells, values, means, hot, pieces, spread)
    wait_for_all(me, got2.at[pl.ds(0, 4 * (DEVICES - 1)), :], sems.at[2], sems.at[3])

    def put(at, value):
        log_perm[:, at : at + 128] = value
        lx[OWN, at : at + 128] = value

    rows_back(got2, row_back, row_turn, put)
    edges = exchange_edges(me, lx.at[pl.ds(8, 8), :], lx.at[pl.ds(16, 8), :], lx, sems.at[pl.ds(8, 4)])
    for copy in edges:
        copy.start()
    for copy in source_edges + edges:
        copy.wait()
    sums = krylov(me, lx, sx, kappa, coefs, diag, v0, z0, z1, z2)
    y = weights(share(me, lane_totals(sums), mine.at[0], everyone.at[0], sems.at[pl.ds(12, 2)]))
    total = spread[...]
    for j in range(TILES):
        p = (y[0] * v0[OWN, tile(j)] + y[1] * z0[OWN, tile(j)]) + (y[2] * z1[OWN, tile(j)] + y[3] * z2[OWN, tile(j)])
        pressure[:, tile(j)] = p
        for g in range(2):
            rows = slice(128 * g + 8 * j, 128 * g + 8 * j + 8)
            off = p[8 * g : 8 * g + 8] - means[rows, :]
            total = total + counts[rows, :128] * (off * off)
    misfit = jnp.sum(total, axis=0, keepdims=True)
    everything = share(me, misfit, mine.at[1], everyone.at[1], sems.at[pl.ds(14, 2)])
    loglik[0, 0] = F32(-2.0 / 8192) * jnp.sum(everything)


def body(state, noise, step, field_scale, wave_scale, source, obs_cells, obs_values):
    vmem = pl.BlockSpec(memory_space=pltpu.VMEM)
    smem = pl.BlockSpec(memory_space=pltpu.SMEM)
    field = pltpu.VMEM((32, N), F32)
    log_perm, pressure, loglik = pl.pallas_call(
        kernel,
        out_shape=(
            jax.ShapeDtypeStruct((FIELD, N), F32),
            jax.ShapeDtypeStruct((FIELD, N), F32),
            jax.ShapeDtypeStruct((1, 1), F32),
        ),
        in_specs=[smem] * 3 + [vmem] * 13,
        out_specs=(vmem, vmem, smem),
        scratch_shapes=[
            pltpu.VMEM((512, 512), BF16),
            pltpu.VMEM((512, 512), BF16),
            pltpu.VMEM((1024, 128), F32),
            pltpu.VMEM((1024, 128), F32),
            pltpu.VMEM((8, KS, 128), F32),
            pltpu.VMEM((512, 128), F32),
            pltpu.VMEM((512, 128), F32),
            pltpu.VMEM((256, 512), F32),
            pltpu.VMEM((256, 128), F32),
            pltpu.VMEM((8, 256, 1024), BF16),
            pltpu.VMEM((512, 1024), BF16),
            pltpu.VMEM((384, 256), BF16),
            pltpu.VMEM((8, 128), F32),
            field,
            field,
            field,
            pltpu.VMEM((4, 32, N), F32),
            pltpu.VMEM((FIELD, N), F32),
            field,
            field,
            field,
            field,
            pltpu.VMEM((2, 8, 128), F32),
            pltpu.VMEM((2, DEVICES, 128), F32),
            pltpu.SemaphoreType.DMA((16,)),
        ],
        compiler_params=pltpu.CompilerParams(collective_id=0, has_side_effects=True, vmem_limit_bytes=60 * 2**20),
    )(
        step, field_scale, wave_scale, state, noise, source,
        obs_cells.reshape(64, 128), obs_values.reshape(64, 128),
        *[jnp.asarray(t) for t in tables()],
    )
    return log_perm, pressure, loglik.reshape(())


def solution(mesh):
    in_specs = (P(AXIS, None), P(AXIS, None), P(), P(), P(), P(AXIS, None), P(), P())
    out_specs = (P(AXIS, None), P(AXIS, None), P())
    return jax.shard_map(body, mesh=mesh, in_specs=in_specs, out_specs=out_specs, check_vma=False)
```

```python
import functools
import math

import jax
import jax.numpy as jnp
import ml_dtypes
import numpy as np
from jax import lax
from jax.experimental import pallas as pl
from jax.experimental.pallas import tpu as pltpu
from jax.sharding import PartitionSpec as P

M = 4096
N = 2048
DEVICES = 128
ROWS = M // DEVICES
FIELD = N // DEVICES
KS = 80
AXIS = "strip"
MESH = pl.DeviceIdType.MESH
F32 = jnp.float32
BF16 = jnp.bfloat16


def halves(table):
    table = table.astype(np.float32)
    high = table.astype(ml_dtypes.bfloat16)
    low = (table - high.astype(np.float32)).astype(ml_dtypes.bfloat16)
    return np.stack([high, low])


def tables():
    b = np.arange(256)
    kl = np.arange(128)
    angle = 2 * np.pi * np.outer(kl, b) / 256
    top = np.zeros((16, 512))
    top[0, :256] = (-1.0) ** b
    row_forward = np.concatenate(
        [
            np.concatenate([np.cos(angle), np.sin(angle)], 1),
            np.concatenate([-np.sin(angle), np.cos(angle)], 1),
            top,
        ]
    )
    row_back = np.concatenate(
        [
            np.concatenate([np.cos(angle), np.sin(angle)], 1),
            np.concatenate([-np.sin(angle), np.cos(angle)], 1),
        ]
    )
    kv = np.arange(16)
    turn = 2 * np.pi * np.outer(kv, b) / M
    row_turn = np.stack([np.cos(turn), np.sin(turn)])
    ks = np.arange(KS)
    real = ks <= 64
    src = np.arange(DEVICES)
    angle = 2 * np.pi * np.outer(ks, src) / 128
    col_forward = np.concatenate([np.cos(angle), -np.sin(angle)]) * np.tile(real, 2)[:, None]
    weight = np.where((ks == 0) | (ks == 64), 1.0, 2.0) * real
    angle = angle.T[:64]
    col_back = np.concatenate([np.cos(angle) * weight, -np.sin(angle) * weight], 1)
    r = np.arange(32)
    lanes_in = [(v, q) for v in range(4) for q in range(32)]
    lanes_out = [(v, h * 8 + q) for h in range(4) for v in range(4) for q in range(8)]
    turn = 2 * np.pi * np.outer(ks, [q for _, q in lanes_in]) / M
    turn_back = 2 * np.pi * np.outer(ks, [q for _, q in lanes_out]) / M
    col_turn = np.stack([np.cos(turn), np.sin(turn), np.cos(turn_back), np.sin(turn_back)])
    vi, qi = np.array(lanes_in).T
    vo, qo = np.array(lanes_out).T
    same = vi[:, None] == vi[None, :]
    angle = 2 * np.pi * qi[:, None] * qi[None, :] / 32
    c, s = np.cos(angle) * same, np.sin(angle) * same
    mid_forward = np.block([[c, -s], [s, c]])
    same = vi[:, None] == vo[None, :]
    angle = 2 * np.pi * qi[:, None] * qo[None, :] / 32
    c, s = np.cos(angle) * same, np.sin(angle) * same
    mid_back = np.block([[c, s], [-s, c]])
    return (
        halves(row_forward),
        halves(row_back),
        row_turn.astype(np.float32),
        halves(col_forward),
        halves(col_back),
        col_turn.astype(np.float32),
        halves(mid_forward),
        halves(mid_back),
    )


def split(x):
    high = x.astype(BF16)
    return high, (x - high.astype(F32)).astype(BF16)


NN = (((1,), (0,)), ((), ()))
NT = (((1,), (1,)), ((), ()))


def product(left, right, form):
    dot = functools.partial(lax.dot_general, dimension_numbers=form, preferred_element_type=F32)
    (lh, ll), (rh, rl) = left, right
    return dot(lh, rh) + (dot(lh, rl) + dot(ll, rh))


def scaled(x, factor):
    if abs(factor) < 1e-12:
        return None
    if abs(factor - 1) < 1e-12:
        return x
    if abs(factor + 1) < 1e-12:
        return -x
    return x * F32(factor)


def plus(a, b):
    return b if a is None else a if b is None else a + b


def minus(a, b):
    if b is None:
        return a
    return -b if a is None else a - b


def turned(z, cos, sin):
    re, im = z
    out_re = scaled(re, cos) if re is not None else None
    out_im = scaled(re, sin) if re is not None else None
    if im is not None:
        out_re = minus(out_re, scaled(im, sin))
        out_im = plus(out_im, scaled(im, cos))
    return out_re, out_im


def added(a, b):
    return plus(a[0], b[0]), plus(a[1], b[1])


def less(a, b):
    return minus(a[0], b[0]), minus(a[1], b[1])


def real_dft(xs):
    count = len(xs)
    if count == 1:
        return [(xs[0], None)]
    even, odd = real_dft(xs[::2]), real_dft(xs[1::2])
    out = [None] * (count // 2 + 1)
    if count == 2:
        return [added(even[0], odd[0]), less(even[0], odd[0])]
    for k in range(count // 4 + 1):
        angle = -2 * math.pi * k / count
        t = turned(odd[k], math.cos(angle), math.sin(angle))
        out[k] = added(even[k], t)
        if k != count // 4:
            re, im = less(even[k], t)
            out[count // 2 - k] = (re, None if im is None else -im)
    return out


def back_dft(zs):
    count = len(zs)
    if count == 1:
        return list(zs)
    even, odd = back_dft(zs[::2]), back_dft(zs[1::2])
    out = [None] * count
    for k in range(count // 2):
        angle = 2 * math.pi * k / count
        t = turned(odd[k], math.cos(angle), math.sin(angle))
        out[k] = added(even[k], t)
        out[k + count // 2] = less(even[k], t)
    return out


def back_dft_real_first_half(zs):
    count = len(zs)
    even, odd = back_dft(zs[::2]), back_dft(zs[1::2])
    out = []
    for k in range(count // 2):
        angle = 2 * math.pi * k / count
        out.append(even[k][0] + turned(odd[k], math.cos(angle), math.sin(angle))[0])
    return out


def send_to_all(me, piece, landing, send_sem, recv_sem):
    @pl.loop(1, DEVICES)
    def _(i):
        other = lax.rem(me + i, DEVICES)
        pltpu.make_async_remote_copy(
            src_ref=piece(other),
            dst_ref=landing(me),
            send_sem=send_sem,
            recv_sem=recv_sem,
            device_id=(other,),
            device_id_type=MESH,
        ).start()


def wait_for_all(me, whole, send_sem, recv_sem):
    pltpu.make_async_remote_copy(
        src_ref=whole,
        dst_ref=whole,
        send_sem=send_sem,
        recv_sem=recv_sem,
        device_id=(lax.rem(me + 1, DEVICES),),
        device_id_type=MESH,
    ).wait()


def greet_all(me):
    barrier = pltpu.get_barrier_semaphore()

    @pl.loop(1, DEVICES)
    def _(i):
        pl.semaphore_signal(barrier, inc=1, device_id=(lax.rem(me + i, DEVICES),), device_id_type=MESH)


def meet_all():
    pl.semaphore_wait(pltpu.get_barrier_semaphore(), DEVICES - 1)


def rows_forward(rate, state, noise, row_turn, z_high, z_low, row_forward, out):
    keep = jnp.sqrt(1.0 - rate * rate)
    for g in range(ROWS // 16):
        rows = slice(16 * g, 16 * g + 16)
        for h in range(2):
            xs = []
            for a in range(16):
                cols = slice(256 * a + 128 * h, 256 * a + 128 * h + 128)
                xs.append(keep * state[rows, cols] + rate * noise[rows, cols])
            ys = real_dft(xs)
            for kv in range(16):
                re, im = ys[kv] if kv <= 8 else ys[16 - kv]
                cos = row_turn[0, kv : kv + 1, 128 * h : 128 * h + 128]
                sin = row_turn[1, kv : kv + 1, 128 * h : 128 * h + 128]
                if kv > 8:
                    im = -im
                if kv == 0:
                    zr, zi = re, jnp.zeros_like(re)
                elif im is None:
                    zr, zi = re * cos, -(re * sin)
                else:
                    zr, zi = re * cos + im * sin, im * cos - re * sin
                spot = slice(kv * ROWS + 16 * g, kv * ROWS + 16 * g + 16)
                for part, lane in ((zr, 128 * h), (zi, 256 + 128 * h)):
                    high, low = split(part)
                    z_high[spot, lane : lane + 128] = high
                    z_low[spot, lane : lane + 128] = low
    for pair in range(2):
        rows = slice(256 * pair, 256 * pair + 256)
        res = product((row_forward[0], row_forward[1]), (z_high[rows, :], z_low[rows, :]), NT)
        for i in range(2):
            t = 2 * pair + i
            lanes = slice(128 * i, 128 * i + 128)
            im = res[128:256, lanes]
            if t == 0:
                first = (lax.broadcasted_iota(jnp.int32, (128, 128), 0) == 0) & (
                    lax.broadcasted_iota(jnp.int32, (128, 128), 1) < ROWS
                )
                im = jnp.where(first, jnp.broadcast_to(res[256:257, lanes], (128, 128)), im)
            out[pl.ds(t, 128, stride=8), :] = res[:128, lanes]
            out[pl.ds(4 + t, 128, stride=8), :] = im


def amplitudes(me, sigma, wave, amp):
    ks = lax.broadcasted_iota(jnp.int32, (KS, 128), 0)
    lane = lax.broadcasted_iota(jnp.int32, (KS, 128), 1)
    k0 = ks + 128 * (lane % 32)
    q0 = jnp.minimum(k0, M - k0).astype(F32)
    base = q0 * q0 + wave * wave
    gain = sigma * wave * F32(2.0 / (math.sqrt(math.pi) * M))
    for v in range(4):
        k1 = 16 * me + 4 * v + lane // 32
        q1 = k1.astype(F32)
        value = gain / (base + q1 * q1)
        if v == 0:
            alone = k1 == 0
            value = jnp.where(alone, 0.5 * value, value)
            top = jnp.where(alone, 0.5 * gain / (base + F32(N) * F32(N)), value)
            amp[4] = top
        else:
            amp[4 + v] = value
        amp[v] = value


def columns(half, got, amp, col_forward, col_back, col_turn, mid_forward, mid_back, out):
    lane = lax.broadcasted_iota(jnp.int32, (64, 128), 1)
    for u in (2 * half, 2 * half + 1):
        pieces = jnp.concatenate([got[pl.ds(2 * u + i, 128, stride=8), :] for i in range(2)], axis=1)
        spec = product((col_forward[0], col_forward[1]), split(pieces), NN)
        parts = []
        for i in range(2):
            lanes = slice(128 * i, 128 * i + 128)
            re, im = spec[:KS, lanes], spec[KS:, lanes]
            cos, sin = col_turn[0], col_turn[1]
            parts.append(jnp.concatenate([re * cos + im * sin, im * cos - re * sin], axis=1))
        full = product(split(jnp.concatenate(parts, axis=0)), (mid_forward[0], mid_forward[1]), NN)
        factor = jnp.concatenate([amp[2 * u], amp[2 * u + 1]], axis=0)
        full = full * jnp.concatenate([factor, factor], axis=1)
        back = product(split(full), (mid_back[0], mid_back[1]), NN)
        sides = []
        for i in range(2):
            rows = slice(KS * i, KS * i + KS)
            re, im = back[rows, :128], back[rows, 128:]
            cos, sin = col_turn[2], col_turn[3]
            sides.append(jnp.concatenate([re * cos - im * sin, im * cos + re * sin], axis=0))
        field = product((col_back[0], col_back[1]), split(jnp.concatenate(sides, axis=1)), NN)
        for i in range(2):
            here = field[:, 128 * i : 128 * i + 128]
            later, sooner = pltpu.roll(here, 32, 1), pltpu.roll(here, 96, 1)
            t = 2 * u + i
            out[pl.ds(t, 64, stride=16), :] = jnp.where(lane < 32, pltpu.roll(later, 1, 0), later)
            out[pl.ds(8 + t, 64, stride=16), :] = jnp.where(lane >= 96, pltpu.roll(sooner, 63, 0), sooner)


def rows_back(got, row_back, row_turn, put):
    blocks = [got[pl.ds(t, 128, stride=8), :].T for t in range(8)]
    row = lax.broadcasted_iota(jnp.int32, (128, 128), 0)
    lane = lax.broadcasted_iota(jnp.int32, (128, 128), 1)
    sign = (1 - 2 * (lane[:8] % 2)).astype(F32)
    tops = [jnp.broadcast_to(blocks[4][32 * g : 32 * g + 8, :1], (8, 128)) * sign for g in range(4)]
    blocks[4] = jnp.where((row % 32 < 8) & (lane == 0), 0.0, blocks[4])
    sides = jnp.concatenate([jnp.concatenate(blocks[:4], axis=0), jnp.concatenate(blocks[4:], axis=0)], axis=1)
    q = product(split(sides), (row_back[0], row_back[1]), NN)
    for h in range(2):
        for g in range(4):
            zs = []
            for kv in range(16):
                at = 128 * (kv // 4) + 32 * g + 8 * (kv % 4)
                rows = slice(at, at + 8)
                zr, zi = q[rows, 128 * h : 128 * h + 128], q[rows, 256 + 128 * h : 384 + 128 * h]
                cos = row_turn[0, kv : kv + 1, 128 * h : 128 * h + 128]
                sin = row_turn[1, kv : kv + 1, 128 * h : 128 * h + 128]
                zs.append((zr, zi) if kv == 0 else (zr * cos - zi * sin, zi * cos + zr * sin))
            for a, value in enumerate(back_dft_real_first_half(zs)):
                put(8 * g, 256 * a + 128 * h, value + tops[g])


def gather_observations(me, cells, values, counts, means, hot, parts):
    counts[...] = jnp.zeros_like(counts)

    @pl.loop(0, 8)
    def _(c):
        for i in range(8):
            cell = cells[pl.ds(8 * c + i, 1), :]
            value = values[pl.ds(8 * c + i, 1), :]
            row = cell // N - FIELD * me
            col = cell % N
            inside = (row >= 0) & (row < FIELD)
            spot = jnp.where(inside, (row // 8) * 128 + (col // 128) * 8 + row % 8, -1)
            lane = jnp.where(inside, col % 128, -1)
            lanes = slice(128 * i, 128 * i + 128)
            here = lax.broadcasted_iota(jnp.int32, (256, 128), 0) == spot
            hot[c, :, lanes] = jnp.where(here, 1.0, 0.0).astype(BF16)
            there = lax.broadcasted_iota(jnp.int32, (128, 128), 0) == lane
            high = value.astype(BF16).astype(F32)
            middle = (value - high).astype(BF16).astype(F32)
            low = value - high - middle
            for j, piece in enumerate((jnp.ones_like(value), high, middle, low)):
                parts[128 * j : 128 * j + 128, lanes] = jnp.where(there, piece, 0.0).astype(BF16)
        counts[...] += lax.dot_general(hot[c], parts[...], NT, preferred_element_type=F32)

    number = counts[:, :128]
    total = counts[:, 128:256] + counts[:, 256:384] + counts[:, 384:]
    means[...] = total / jnp.maximum(number, 1.0)


def spread_observations(me, cells, values, means, hot, pieces, spread):
    turned_means = jnp.concatenate([means[:128, :].T, means[128:, :].T], axis=1)
    high = turned_means.astype(BF16)
    rest = turned_means - high.astype(F32)
    middle = rest.astype(BF16)
    pieces[:128, :] = high
    pieces[128:256, :] = middle
    pieces[256:, :] = (rest - middle.astype(F32)).astype(BF16)
    spread[...] = jnp.zeros_like(spread)

    @pl.loop(0, 8)
    def _(c):
        picked = jnp.dot(pieces[...], hot[c], preferred_element_type=F32)
        total = jnp.zeros((8, 128), F32)
        for i in range(8):
            cell = cells[pl.ds(8 * c + i, 1), :]
            value = values[pl.ds(8 * c + i, 1), :]
            row = cell // N - FIELD * me
            inside = (row >= 0) & (row < FIELD)
            lane = jnp.where(inside, cell % 128, -1)
            lanes = slice(128 * i, 128 * i + 128)
            mean = picked[:128, lanes] + (picked[128:256, lanes] + picked[256:, lanes])
            there = lax.broadcasted_iota(jnp.int32, (128, 128), 0) == lane
            off = jnp.where(there, value - mean, 0.0)
            off = off * off
            for k in range(16):
                total = total + off[8 * k : 8 * k + 8]
        spread[...] += total


def exchange_edges(me, own_low, own_high, ext, sems):
    up, down = lax.rem(me + 1, DEVICES), lax.rem(me + DEVICES - 1, DEVICES)
    return [
        pltpu.make_async_remote_copy(
            src_ref=own_low, dst_ref=ext.at[pl.ds(24, 8), :], send_sem=sems.at[0], recv_sem=sems.at[1],
            device_id=(down,), device_id_type=MESH,
        ),
        pltpu.make_async_remote_copy(
            src_ref=own_high, dst_ref=ext.at[pl.ds(0, 8), :], send_sem=sems.at[2], recv_sem=sems.at[3],
            device_id=(up,), device_id_type=MESH,
        ),
    ]


TILES = N // 128
OWN = slice(8, 24)


def tile(j):
    return slice(128 * j, 128 * j + 128)


def neighbours(load):
    lane = lax.broadcasted_iota(jnp.int32, (32, 128), 1)
    values = [load(0), load(1)]
    rights = [pltpu.roll(v, 1, 1) for v in values]
    lefts = [pltpu.roll(v, 127, 1) for v in values]
    before = jnp.zeros_like(rights[0])
    for j in range(TILES):
        if j == TILES - 1:
            after = jnp.zeros_like(before)
        else:
            after = lefts[1]
        west = jnp.where(lane == 0, before, rights[0])
        east = jnp.where(lane == 127, after, lefts[0])
        north = pltpu.roll(values[0], 1, 0)
        south = pltpu.roll(values[0], 31, 0)
        yield j, values[0], north, south, west, east
        before = rights[0]
        if j + 1 < TILES:
            values = values[1:]
            rights = rights[1:]
            lefts = lefts[1:]
            if j + 2 < TILES:
                values.append(load(j + 2))
                rights.append(pltpu.roll(values[1], 1, 1))
                lefts.append(pltpu.roll(values[1], 127, 1))


def krylov(me, lx, sx, kappa, coefs, diag, v0, z0, z1, z2):
    row = lax.broadcasted_iota(jnp.int32, (32, 128), 0)
    lane = lax.broadcasted_iota(jnp.int32, (32, 128), 1)
    valid = ((row >= 8) | (me > 0)) & ((row < 24) | (me < DEVICES - 1))
    for j in range(TILES):
        kappa[:, tile(j)] = jnp.where(valid, jnp.exp(lx[:, tile(j)]), 0.0)
    sums = [jnp.zeros((16, 128), F32) for _ in range(8)]
    for j, k, kn, ks, kw, ke in neighbours(lambda j: kappa[:, tile(j)]):
        north, south, west, east = 0.5 * (k + kn), 0.5 * (k + ks), 0.5 * (k + kw), 0.5 * (k + ke)
        d = north + south + west + east
        inverse = jnp.where(valid, 1.0 / d, 0.0)
        coefs[0, :, tile(j)] = north * inverse
        coefs[1, :, tile(j)] = south * inverse
        coefs[2, :, tile(j)] = west * inverse
        coefs[3, :, tile(j)] = east * inverse
        source = sx[:, tile(j)]
        first = source * inverse
        diag[:, tile(j)] = d[OWN]
        v0[:, tile(j)] = first
        sums[0] = sums[0] + source[OWN] * first[OWN]

    def beside(values):
        for j, v, vn, vs, vw, ve in neighbours(lambda j: values[:, tile(j)]):
            yield j, v, (coefs[0, :, tile(j)] * vn + coefs[1, :, tile(j)] * vs) + (
                coefs[2, :, tile(j)] * vw + coefs[3, :, tile(j)] * ve
            )

    for j, v, s in beside(v0):
        z = v - s
        z0[:, tile(j)] = z
        own = z[OWN]
        sums[1] = sums[1] + sx[OWN, tile(j)] * own
        sums[2] = sums[2] + diag[:, tile(j)] * own * own
    for j, v, s in beside(z0):
        z = -s
        z1[:, tile(j)] = z
        own = diag[:, tile(j)] * z[OWN]
        sums[3] = sums[3] + own * v[OWN]
        sums[4] = sums[4] + own * z[OWN]
    for j, v, s in beside(z1):
        z = -2.0 * s - z0[:, tile(j)]
        z2[:, tile(j)] = z
        own = diag[:, tile(j)] * z[OWN]
        sums[5] = sums[5] + own * v[OWN]
        sums[6] = sums[6] + own * z[OWN]
    for j, v, s in beside(z2):
        z = -2.0 * s[OWN] - z1[OWN, tile(j)]
        sums[7] = sums[7] + diag[:, tile(j)] * v[OWN] * z
    return sums


def lane_totals(sums):
    count = len(sums)
    high = -(-count // 8) * 8
    rows = [jnp.sum(s, axis=0, keepdims=True) for s in sums] + [jnp.zeros((1, 128), F32)] * (high - count)
    rows = jnp.concatenate(rows, axis=0)
    totals = jnp.broadcast_to(jnp.sum(rows, axis=1, keepdims=True), (high, 128))
    at = lax.broadcasted_iota(jnp.int32, (high, 128), 0) == lax.broadcasted_iota(jnp.int32, (high, 128), 1)
    return jnp.sum(jnp.where(at, totals, 0.0), axis=0, keepdims=True)


def share(me, row, mine, all_rows, sems):
    mine[0:1, :] = row
    all_rows[pl.ds(me, 1), :] = row
    send_to_all(me, lambda d: mine.at[pl.ds(0, 1), :], lambda s: all_rows.at[pl.ds(s, 1), :], sems.at[0], sems.at[1])


def shared(me, all_rows, sems):
    wait_for_all(me, all_rows.at[pl.ds(0, DEVICES - 1), :], sems.at[0], sems.at[1])


PAIRS = [(i, j) for i in range(4) for j in range(i, 4)]


def misfit_parts(guess, fields, counts, means, spread):
    sums = [spread[...]] + [jnp.zeros((8, 128), F32) for _ in range(14)]
    for j in range(TILES):
        for g in range(2):
            rows = slice(128 * g + 8 * j, 128 * g + 8 * j + 8)
            us = [f[8 + 8 * g : 16 + 8 * g, tile(j)] for f in fields]
            n = counts[rows, :128]
            off = ((guess[0] * us[0] + guess[1] * us[1]) + (guess[2] * us[2] + guess[3] * us[3])) - means[rows, :]
            many = n * off
            sums[0] = sums[0] + many * off
            for i in range(4):
                sums[1 + i] = sums[1 + i] + many * us[i]
            scaled_us = [n * u for u in us]
            for k, (i, l) in enumerate(PAIRS):
                sums[5 + k] = sums[5 + k] + scaled_us[i] * us[l]
    row = lane_totals(sums)
    lane = lax.broadcasted_iota(jnp.int32, (1, 128), 1)
    for i in range(4):
        row = jnp.where(lane == 15 + i, guess[i][:1], row)
    return row


def misfit(y, rows):
    table = rows.T
    off = [y[i][:1] - table[15 + i : 16 + i] for i in range(4)]
    total = table[0:1]
    for i in range(4):
        total = total + 2.0 * off[i] * table[1 + i : 2 + i]
    for k, (i, l) in enumerate(PAIRS):
        term = off[i] * off[l] * table[5 + k : 6 + k]
        total = total + (term if i == l else 2.0 * term)
    return jnp.sum(total)


def weights(row):
    take = [jnp.broadcast_to(row[:, i : i + 1], (8, 128)) for i in range(8)]
    g0, e0, m0, m1, q11, q12, q22, q23 = take
    m2 = 2.0 * q11 - m0
    m3 = 2.0 * q12 - m1
    m4 = 2.0 * q22 - m0
    m5 = 2.0 * q23 - m1
    m = [m0, m1, m2, m3, m4, m5]

    def inner(i, j):
        return 0.5 * (m[i + j] + m[abs(i - j)])

    def energy(i, j):
        return inner(i, j) + 0.5 * (inner(i, j + 1) + inner(i, abs(j - 1)))

    gram = [[None] * 4 for _ in range(4)]
    gram[0][0] = e0
    for j in range(3):
        gram[j + 1][0] = inner(0, j)
        for i in range(j + 1):
            gram[j + 1][i + 1] = energy(i, j)
    right = [g0, e0, m0 - e0, 2.0 * (m1 - (m0 - e0)) - e0]
    factors = [[None] * 4 for _ in range(4)]
    inverse = []
    whole = [gram[i][i] for i in range(4)]
    for k in range(4):
        pivot = gram[k][k]
        inverse.append(jnp.where(pivot > 1e-6 * whole[k], 1.0 / pivot, 0.0))
        for i in range(k + 1, 4):
            factors[i][k] = gram[i][k] * inverse[k]
        for i in range(k + 1, 4):
            for j in range(k + 1, i + 1):
                gram[i][j] = gram[i][j] - factors[i][k] * gram[j][k]
            right[i] = right[i] - factors[i][k] * right[k]
    out = [right[k] * inverse[k] for k in range(4)]
    for k in (2, 1, 0):
        for i in range(k + 1, 4):
            out[k] = out[k] - factors[i][k] * out[i]
    return out


LOADS = ("state", "noise", "source", "cells", "values",
         "row_forward", "row_back", "row_turn", "col_forward", "col_back", "col_turn", "mid_forward", "mid_back")


def kernel(*refs):
    (step, sigma, wave), refs = refs[:3], refs[3:]
    count = len(LOADS)
    sources, refs = refs[:count], refs[count:]
    (log_perm_out, pressure_out, loglik), refs = refs[:3], refs[3:]
    held, refs = refs[:count], refs[count:]
    (
        z_high, z_low, sent1, got1, amp, sent2, got2,
        counts, means, hot, parts, pieces, spread,
        lx, sx, kappa, coefs, diag, v0, z0, z1, z2, mine, everyone, pressure, sems, load_sems,
    ) = refs
    me = lax.axis_index(AXIS)
    loads = {
        name: pltpu.make_async_copy(sources[k], held[k], load_sems.at[k]) for k, name in enumerate(LOADS)
    }
    for name in LOADS:
        loads[name].start()
    (state, noise, source, cells, values,
     row_forward, row_back, row_turn, col_forward, col_back, col_turn, mid_forward, mid_back) = held
    greet_all(me)
    for name in ("state", "noise", "row_turn", "row_forward"):
        loads[name].wait()
    rows_forward(step[0], state, noise, row_turn, z_high, z_low, row_forward, sent1)
    loads["source"].wait()
    meet_all()
    for half in range(2):
        send_to_all(
            me, lambda d: sent1.at[pl.ds(8 * d + 4 * half, 4), :], lambda s: got1.at[pl.ds(8 * s + 4 * half, 4), :],
            sems.at[2 * half], sems.at[2 * half + 1],
        )
    source_edges = exchange_edges(me, source.at[pl.ds(0, 8), :], source.at[pl.ds(8, 8), :], sx, sems.at[pl.ds(8, 4)])
    for copy in source_edges:
        copy.start()
    own = pl.ds(pl.multiple_of(8 * me, 8), 8)
    got1[own, :] = sent1[own, :]
    sx[OWN, :] = source[...]
    amplitudes(me, sigma[0], wave[0], amp)
    loads["cells"].wait()
    loads["values"].wait()
    gather_observations(me, cells, values, counts, means, hot, parts)
    for name in ("col_forward", "col_back", "col_turn", "mid_forward", "mid_back", "row_back"):
        loads[name].wait()
    for half in range(2):
        wait_for_all(me, got1.at[pl.ds(0, 4 * (DEVICES - 1)), :], sems.at[2 * half], sems.at[2 * half + 1])
        columns(half, got1, amp, col_forward, col_back, col_turn, mid_forward, mid_back, sent2)
        send_to_all(
            me, lambda d: sent2.at[pl.ds(8 * d + 4 * half, 4), :], lambda s: got2.at[pl.ds(8 * s + 4 * half, 4), :],
            sems.at[4 + 2 * half], sems.at[5 + 2 * half],
        )
    got2[own, :] = sent2[own, :]
    spread_observations(me, cells, values, means, hot, pieces, spread)
    for half in range(2):
        wait_for_all(me, got2.at[pl.ds(0, 4 * (DEVICES - 1)), :], sems.at[4 + 2 * half], sems.at[5 + 2 * half])

    def put(row, at, value):
        lx[row : row + 8, at : at + 128] = value

    rows_back(got2, row_back, row_turn, put)
    write = pltpu.make_async_copy(lx.at[pl.ds(8, FIELD), :], log_perm_out, load_sems.at[count])
    write.start()
    for copy in source_edges:
        copy.wait()
    sums = krylov(me, lx, sx, kappa, coefs, diag, v0, z0, z1, z2)
    row = lane_totals(sums)
    share(me, row, mine.at[0], everyone.at[0], sems.at[pl.ds(12, 2)])
    fields = (v0, z0, z1, z2)
    guess = weights(row)
    fine = jnp.abs(guess[0]) < 64.0
    for i in range(1, 4):
        fine = fine & (jnp.abs(guess[i]) < 64.0)
    guess = [jnp.where(fine, g, 0.0) for g in guess]
    share(me, misfit_parts(guess, fields, counts, means, spread), mine.at[1], everyone.at[1], sems.at[pl.ds(14, 2)])
    shared(me, everyone.at[0], sems.at[pl.ds(12, 2)])
    y = weights(jnp.sum(everyone[0], axis=0, keepdims=True))
    for j in range(TILES):
        for g in range(2):
            us = [f[8 + 8 * g : 16 + 8 * g, tile(j)] for f in fields]
            pressure[8 * g : 8 * g + 8, tile(j)] = (y[0] * us[0] + y[1] * us[1]) + (y[2] * us[2] + y[3] * us[3])
    write_pressure = pltpu.make_async_copy(pressure, pressure_out, load_sems.at[count + 1])
    write_pressure.start()
    shared(me, everyone.at[1], sems.at[pl.ds(14, 2)])
    loglik[0, 0] = F32(-2.0 / 8192) * misfit(y, everyone[1])
    write.wait()
    write_pressure.wait()


def body(state, noise, step, field_scale, wave_scale, source, obs_cells, obs_values):
    anywhere = pl.BlockSpec(memory_space=pl.ANY)
    smem = pl.BlockSpec(memory_space=pltpu.SMEM)
    field = pltpu.VMEM((32, N), F32)
    own = pltpu.VMEM((FIELD, N), F32)
    arrays = [state, noise, source, obs_cells.reshape(64, 128), obs_values.reshape(64, 128)]
    arrays += [jnp.asarray(t) for t in tables()]
    log_perm, pressure, loglik = pl.pallas_call(
        kernel,
        out_shape=(
            jax.ShapeDtypeStruct((FIELD, N), F32),
            jax.ShapeDtypeStruct((FIELD, N), F32),
            jax.ShapeDtypeStruct((1, 1), F32),
        ),
        in_specs=[pl.BlockSpec(memory_space=pltpu.SMEM)] * 3 + [anywhere] * len(arrays),
        out_specs=(anywhere, anywhere, smem),
        scratch_shapes=[
            pltpu.VMEM(a.shape, a.dtype) for a in arrays
        ] + [
            pltpu.VMEM((512, 512), BF16),
            pltpu.VMEM((512, 512), BF16),
            pltpu.VMEM((1024, 128), F32),
            pltpu.VMEM((1024, 128), F32),
            pltpu.VMEM((8, KS, 128), F32),
            pltpu.VMEM((1024, 128), F32),
            pltpu.VMEM((1024, 128), F32),
            pltpu.VMEM((256, 512), F32),
            pltpu.VMEM((256, 128), F32),
            pltpu.VMEM((8, 256, 1024), BF16),
            pltpu.VMEM((512, 1024), BF16),
            pltpu.VMEM((384, 256), BF16),
            pltpu.VMEM((8, 128), F32),
            field,
            field,
            field,
            pltpu.VMEM((4, 32, N), F32),
            own,
            field,
            field,
            field,
            field,
            pltpu.VMEM((2, 8, 128), F32),
            pltpu.VMEM((2, DEVICES, 128), F32),
            own,
            pltpu.SemaphoreType.DMA((16,)),
            pltpu.SemaphoreType.DMA((len(arrays) + 2,)),
        ],
        compiler_params=pltpu.CompilerParams(collective_id=0, has_side_effects=True, vmem_limit_bytes=40 * 2**20),
    )(step, field_scale, wave_scale, *[pltpu.with_memory_space_constraint(a, pltpu.HBM) for a in arrays])
    return log_perm, pressure, loglik.reshape(())


def solution(mesh):
    in_specs = (P(AXIS, None), P(AXIS, None), P(), P(), P(), P(AXIS, None), P(), P())
    out_specs = (P(AXIS, None), P(AXIS, None), P())
    return jax.shard_map(body, mesh=mesh, in_specs=in_specs, out_specs=out_specs, check_vma=False)
```

```python
import functools
import math

import jax
import jax.numpy as jnp
import ml_dtypes
import numpy as np
from jax import lax
from jax.experimental import pallas as pl
from jax.experimental.pallas import tpu as pltpu
from jax.sharding import PartitionSpec as P

M = 4096
N = 2048
DEVICES = 128
ROWS = M // DEVICES
FIELD = N // DEVICES
KS = 80
PARTS = 2
PIECE = 8 // PARTS
AXIS = "strip"
MESH = pl.DeviceIdType.MESH
F32 = jnp.float32
BF16 = jnp.bfloat16


def halves(table):
    table = table.astype(np.float32)
    high = table.astype(ml_dtypes.bfloat16)
    low = (table - high.astype(np.float32)).astype(ml_dtypes.bfloat16)
    return np.stack([high, low])


def tables():
    b = np.arange(256)
    kl = np.arange(128)
    angle = 2 * np.pi * np.outer(kl, b) / 256
    top = np.zeros((16, 512))
    top[0, :256] = (-1.0) ** b
    row_forward = np.concatenate(
        [
            np.concatenate([np.cos(angle), np.sin(angle)], 1),
            np.concatenate([-np.sin(angle), np.cos(angle)], 1),
            top,
        ]
    )
    row_back = np.concatenate(
        [
            np.concatenate([np.cos(angle), np.sin(angle)], 1),
            np.concatenate([-np.sin(angle), np.cos(angle)], 1),
        ]
    )
    kv = np.arange(16)
    turn = 2 * np.pi * np.outer(kv, b) / M
    row_turn = np.stack([np.cos(turn), np.sin(turn)])
    ks = np.arange(KS)
    real = ks <= 64
    src = np.arange(DEVICES)
    angle = 2 * np.pi * np.outer(ks, src) / 128
    col_forward = np.concatenate([np.cos(angle), -np.sin(angle)]) * np.tile(real, 2)[:, None]
    weight = np.where((ks == 0) | (ks == 64), 1.0, 2.0) * real
    angle = angle.T[:64]
    col_back = np.concatenate([np.cos(angle) * weight, -np.sin(angle) * weight], 1)
    r = np.arange(32)
    lanes_in = [(v, q) for v in range(4) for q in range(32)]
    lanes_out = [(v, h * 8 + q) for h in range(4) for v in range(4) for q in range(8)]
    turn = 2 * np.pi * np.outer(ks, [q for _, q in lanes_in]) / M
    turn_back = 2 * np.pi * np.outer(ks, [q for _, q in lanes_out]) / M
    col_turn = np.stack([np.cos(turn), np.sin(turn), np.cos(turn_back), np.sin(turn_back)])
    vi, qi = np.array(lanes_in).T
    vo, qo = np.array(lanes_out).T
    same = vi[:, None] == vi[None, :]
    angle = 2 * np.pi * qi[:, None] * qi[None, :] / 32
    c, s = np.cos(angle) * same, np.sin(angle) * same
    mid_forward = np.block([[c, -s], [s, c]])
    same = vi[:, None] == vo[None, :]
    angle = 2 * np.pi * qi[:, None] * qo[None, :] / 32
    c, s = np.cos(angle) * same, np.sin(angle) * same
    mid_back = np.block([[c, s], [-s, c]])
    return (
        halves(row_forward),
        halves(row_back),
        row_turn.astype(np.float32),
        halves(col_forward),
        halves(col_back),
        col_turn.astype(np.float32),
        halves(mid_forward),
        halves(mid_back),
    )


def split(x):
    high = x.astype(BF16)
    return high, (x - high.astype(F32)).astype(BF16)


NN = (((1,), (0,)), ((), ()))
NT = (((1,), (1,)), ((), ()))


def product(left, right, form):
    (lh, ll), (rh, rl) = left, right
    axis_left, axis_right = form[0][0][0], form[0][1][0]
    return lax.dot_general(
        jnp.concatenate([lh, lh, ll], axis=axis_left),
        jnp.concatenate([rh, rl, rh], axis=axis_right),
        dimension_numbers=form,
        preferred_element_type=F32,
    )


def scaled(x, factor):
    if abs(factor) < 1e-12:
        return None
    if abs(factor - 1) < 1e-12:
        return x
    if abs(factor + 1) < 1e-12:
        return -x
    return x * F32(factor)


def plus(a, b):
    return b if a is None else a if b is None else a + b


def minus(a, b):
    if b is None:
        return a
    return -b if a is None else a - b


def turned(z, cos, sin):
    re, im = z
    out_re = scaled(re, cos) if re is not None else None
    out_im = scaled(re, sin) if re is not None else None
    if im is not None:
        out_re = minus(out_re, scaled(im, sin))
        out_im = plus(out_im, scaled(im, cos))
    return out_re, out_im


def added(a, b):
    return plus(a[0], b[0]), plus(a[1], b[1])


def less(a, b):
    return minus(a[0], b[0]), minus(a[1], b[1])


def real_dft(xs):
    count = len(xs)
    if count == 1:
        return [(xs[0], None)]
    even, odd = real_dft(xs[::2]), real_dft(xs[1::2])
    out = [None] * (count // 2 + 1)
    if count == 2:
        return [added(even[0], odd[0]), less(even[0], odd[0])]
    for k in range(count // 4 + 1):
        angle = -2 * math.pi * k / count
        t = turned(odd[k], math.cos(angle), math.sin(angle))
        out[k] = added(even[k], t)
        if k != count // 4:
            re, im = less(even[k], t)
            out[count // 2 - k] = (re, None if im is None else -im)
    return out


def back_dft(zs):
    count = len(zs)
    if count == 1:
        return list(zs)
    even, odd = back_dft(zs[::2]), back_dft(zs[1::2])
    out = [None] * count
    for k in range(count // 2):
        angle = 2 * math.pi * k / count
        t = turned(odd[k], math.cos(angle), math.sin(angle))
        out[k] = added(even[k], t)
        out[k + count // 2] = less(even[k], t)
    return out


def back_dft_real_first_half(zs):
    count = len(zs)
    even, odd = back_dft(zs[::2]), back_dft(zs[1::2])
    out = []
    for k in range(count // 2):
        angle = 2 * math.pi * k / count
        out.append(even[k][0] + turned(odd[k], math.cos(angle), math.sin(angle))[0])
    return out


def send_to_all(me, piece, landing, send_sem, recv_sem):
    for i in range(1, DEVICES):
        other = me + i
        other = jnp.where(other >= DEVICES, other - DEVICES, other)
        pltpu.make_async_remote_copy(
            src_ref=piece(other),
            dst_ref=landing(me),
            send_sem=send_sem,
            recv_sem=recv_sem,
            device_id=(other,),
            device_id_type=MESH,
        ).start()


def wait_for_all(me, whole, send_sem, recv_sem):
    pltpu.make_async_remote_copy(
        src_ref=whole,
        dst_ref=whole,
        send_sem=send_sem,
        recv_sem=recv_sem,
        device_id=(lax.rem(me + 1, DEVICES),),
        device_id_type=MESH,
    ).wait()


def greet_all(me):
    barrier = pltpu.get_barrier_semaphore()

    @pl.loop(1, DEVICES)
    def _(i):
        pl.semaphore_signal(barrier, inc=1, device_id=(lax.rem(me + i, DEVICES),), device_id_type=MESH)


def meet_all():
    pl.semaphore_wait(pltpu.get_barrier_semaphore(), DEVICES - 1)


def rows_forward(rate, state, noise, row_turn, z_high, z_low, row_forward, out):
    keep = jnp.sqrt(1.0 - rate * rate)
    for g in range(ROWS // 16):
        rows = slice(16 * g, 16 * g + 16)
        for h in range(2):
            xs = []
            for a in range(16):
                cols = slice(256 * a + 128 * h, 256 * a + 128 * h + 128)
                xs.append(keep * state[rows, cols] + rate * noise[rows, cols])
            ys = real_dft(xs)
            for kv in range(16):
                re, im = ys[kv] if kv <= 8 else ys[16 - kv]
                cos = row_turn[0, kv : kv + 1, 128 * h : 128 * h + 128]
                sin = row_turn[1, kv : kv + 1, 128 * h : 128 * h + 128]
                if kv > 8:
                    im = -im
                if kv == 0:
                    zr, zi = re, jnp.zeros_like(re)
                elif im is None:
                    zr, zi = re * cos, -(re * sin)
                else:
                    zr, zi = re * cos + im * sin, im * cos - re * sin
                spot = slice(kv * ROWS + 16 * g, kv * ROWS + 16 * g + 16)
                for part, lane in ((zr, 128 * h), (zi, 256 + 128 * h)):
                    high, low = split(part)
                    z_high[spot, lane : lane + 128] = high
                    z_low[spot, lane : lane + 128] = low
    for pair in range(2):
        rows = slice(256 * pair, 256 * pair + 256)
        res = product((row_forward[0], row_forward[1]), (z_high[rows, :], z_low[rows, :]), NT)
        for i in range(2):
            t = 2 * pair + i
            lanes = slice(128 * i, 128 * i + 128)
            im = res[128:256, lanes]
            if t == 0:
                first = (lax.broadcasted_iota(jnp.int32, (128, 128), 0) == 0) & (
                    lax.broadcasted_iota(jnp.int32, (128, 128), 1) < ROWS
                )
                im = jnp.where(first, jnp.broadcast_to(res[256:257, lanes], (128, 128)), im)
            out[pl.ds(t, 128, stride=8), :] = res[:128, lanes]
            out[pl.ds(4 + t, 128, stride=8), :] = im


def amplitudes(me, sigma, wave, amp):
    ks = lax.broadcasted_iota(jnp.int32, (KS, 128), 0)
    lane = lax.broadcasted_iota(jnp.int32, (KS, 128), 1)
    k0 = ks + 128 * (lane % 32)
    q0 = jnp.minimum(k0, M - k0).astype(F32)
    base = q0 * q0 + wave * wave
    gain = sigma * wave * F32(2.0 / (math.sqrt(math.pi) * M))
    for v in range(4):
        k1 = 16 * me + 4 * v + lane // 32
        q1 = k1.astype(F32)
        value = gain / (base + q1 * q1)
        if v == 0:
            alone = k1 == 0
            value = jnp.where(alone, 0.5 * value, value)
            top = jnp.where(alone, 0.5 * gain / (base + F32(N) * F32(N)), value)
            amp[4] = top
        else:
            amp[4 + v] = value
        amp[v] = value


def columns(part, got, amp, col_forward, col_back, col_turn, mid_forward, mid_back, out):
    lane = lax.broadcasted_iota(jnp.int32, (64, 128), 1)
    for u in range(4 // PARTS * part, 4 // PARTS * (part + 1)):
        pieces = jnp.concatenate([got[pl.ds(2 * u + i, 128, stride=8), :] for i in range(2)], axis=1)
        spec = product((col_forward[0], col_forward[1]), split(pieces), NN)
        parts = []
        for i in range(2):
            lanes = slice(128 * i, 128 * i + 128)
            re, im = spec[:KS, lanes], spec[KS:, lanes]
            cos, sin = col_turn[0], col_turn[1]
            parts.append(jnp.concatenate([re * cos + im * sin, im * cos - re * sin], axis=1))
        full = product(split(jnp.concatenate(parts, axis=0)), (mid_forward[0], mid_forward[1]), NN)
        factor = jnp.concatenate([amp[2 * u], amp[2 * u + 1]], axis=0)
        full = full * jnp.concatenate([factor, factor], axis=1)
        back = product(split(full), (mid_back[0], mid_back[1]), NN)
        sides = []
        for i in range(2):
            rows = slice(KS * i, KS * i + KS)
            re, im = back[rows, :128], back[rows, 128:]
            cos, sin = col_turn[2], col_turn[3]
            sides.append(jnp.concatenate([re * cos - im * sin, im * cos + re * sin], axis=0))
        field = product((col_back[0], col_back[1]), split(jnp.concatenate(sides, axis=1)), NN)
        for i in range(2):
            here = field[:, 128 * i : 128 * i + 128]
            later, sooner = pltpu.roll(here, 32, 1), pltpu.roll(here, 96, 1)
            t = 2 * u + i
            out[pl.ds(t, 64, stride=16), :] = jnp.where(lane < 32, pltpu.roll(later, 1, 0), later)
            out[pl.ds(8 + t, 64, stride=16), :] = jnp.where(lane >= 96, pltpu.roll(sooner, 63, 0), sooner)


def rows_back(got, row_back, row_turn, put):
    blocks = [got[pl.ds(t, 128, stride=8), :].T for t in range(8)]
    row = lax.broadcasted_iota(jnp.int32, (128, 128), 0)
    lane = lax.broadcasted_iota(jnp.int32, (128, 128), 1)
    sign = (1 - 2 * (lane[:8] % 2)).astype(F32)
    tops = [jnp.broadcast_to(blocks[4][32 * g : 32 * g + 8, :1], (8, 128)) * sign for g in range(4)]
    blocks[4] = jnp.where((row % 32 < 8) & (lane == 0), 0.0, blocks[4])
    sides = jnp.concatenate([jnp.concatenate(blocks[:4], axis=0), jnp.concatenate(blocks[4:], axis=0)], axis=1)
    q = product(split(sides), (row_back[0], row_back[1]), NN)
    for h in range(2):
        for g in range(4):
            zs = []
            for kv in range(16):
                at = 128 * (kv // 4) + 32 * g + 8 * (kv % 4)
                rows = slice(at, at + 8)
                zr, zi = q[rows, 128 * h : 128 * h + 128], q[rows, 256 + 128 * h : 384 + 128 * h]
                cos = row_turn[0, kv : kv + 1, 128 * h : 128 * h + 128]
                sin = row_turn[1, kv : kv + 1, 128 * h : 128 * h + 128]
                zs.append((zr, zi) if kv == 0 else (zr * cos - zi * sin, zi * cos + zr * sin))
            for a, value in enumerate(back_dft_real_first_half(zs)):
                put(8 * g, 256 * a + 128 * h, value + tops[g])


def gather_observations(me, cells, values, counts, means, hot, parts):
    counts[...] = jnp.zeros_like(counts)

    @pl.loop(0, 8)
    def _(c):
        for i in range(8):
            cell = cells[pl.ds(8 * c + i, 1), :]
            value = values[pl.ds(8 * c + i, 1), :]
            row = cell // N - FIELD * me
            col = cell % N
            inside = (row >= 0) & (row < FIELD)
            spot = jnp.where(inside, (row // 8) * 128 + (col // 128) * 8 + row % 8, -1)
            lane = jnp.where(inside, col % 128, -1)
            lanes = slice(128 * i, 128 * i + 128)
            here = lax.broadcasted_iota(jnp.int32, (256, 128), 0) == spot
            hot[c, :, lanes] = jnp.where(here, 1.0, 0.0).astype(BF16)
            there = lax.broadcasted_iota(jnp.int32, (128, 128), 0) == lane
            high = value.astype(BF16).astype(F32)
            middle = (value - high).astype(BF16).astype(F32)
            low = value - high - middle
            for j, piece in enumerate((jnp.ones_like(value), high, middle, low)):
                parts[128 * j : 128 * j + 128, lanes] = jnp.where(there, piece, 0.0).astype(BF16)
        counts[...] += lax.dot_general(hot[c], parts[...], NT, preferred_element_type=F32)

    number = counts[:, :128]
    total = counts[:, 128:256] + counts[:, 256:384] + counts[:, 384:]
    means[...] = total / jnp.maximum(number, 1.0)


def spread_observations(me, cells, values, means, hot, spread):
    turned_means = jnp.concatenate([means[:128, :].T, means[128:, :].T], axis=1)
    pieces = jnp.concatenate(split(turned_means), axis=0)
    spread[...] = jnp.zeros_like(spread)

    @pl.loop(0, 8)
    def _(c):
        totals = [jnp.zeros((8, 128), F32) for _ in range(4)]
        for b in range(4):
            picked = jnp.dot(pieces, hot[c, :, 256 * b : 256 * b + 256], preferred_element_type=F32)
            for i in range(2):
                cell = cells[pl.ds(8 * c + 2 * b + i, 1), :]
                value = values[pl.ds(8 * c + 2 * b + i, 1), :]
                row = cell // N - FIELD * me
                lane = jnp.where((row >= 0) & (row < FIELD), cell % 128, -1)
                lanes = slice(128 * i, 128 * i + 128)
                mean = picked[:128, lanes] + picked[128:, lanes]
                there = lax.broadcasted_iota(jnp.int32, (128, 128), 0) == lane
                off = jnp.where(there, value - mean, 0.0)
                off = off * off
                for k in range(16):
                    totals[k % 4] = totals[k % 4] + off[8 * k : 8 * k + 8]
        spread[...] += (totals[0] + totals[1]) + (totals[2] + totals[3])


def exchange_edges(me, own_low, own_high, ext, sems):
    up, down = lax.rem(me + 1, DEVICES), lax.rem(me + DEVICES - 1, DEVICES)
    return [
        pltpu.make_async_remote_copy(
            src_ref=own_low, dst_ref=ext.at[pl.ds(24, 8), :], send_sem=sems.at[0], recv_sem=sems.at[1],
            device_id=(down,), device_id_type=MESH,
        ),
        pltpu.make_async_remote_copy(
            src_ref=own_high, dst_ref=ext.at[pl.ds(0, 8), :], send_sem=sems.at[2], recv_sem=sems.at[3],
            device_id=(up,), device_id_type=MESH,
        ),
    ]


TILES = N // 128
OWN = slice(8, 24)


def tile(j):
    return slice(128 * j, 128 * j + 128)


def neighbours(load):
    lane = lax.broadcasted_iota(jnp.int32, (32, 128), 1)
    values = [load(0), load(1)]
    rights = [pltpu.roll(v, 1, 1) for v in values]
    lefts = [pltpu.roll(v, 127, 1) for v in values]
    before = jnp.zeros_like(rights[0])
    for j in range(TILES):
        if j == TILES - 1:
            after = jnp.zeros_like(before)
        else:
            after = lefts[1]
        west = jnp.where(lane == 0, before, rights[0])
        east = jnp.where(lane == 127, after, lefts[0])
        north = pltpu.roll(values[0], 1, 0)
        south = pltpu.roll(values[0], 31, 0)
        yield j, values[0], north, south, west, east
        before = rights[0]
        if j + 1 < TILES:
            values = values[1:]
            rights = rights[1:]
            lefts = lefts[1:]
            if j + 2 < TILES:
                values.append(load(j + 2))
                rights.append(pltpu.roll(values[1], 1, 1))
                lefts.append(pltpu.roll(values[1], 127, 1))


def krylov(me, lx, sx, kappa, coefs, diag, v0, z0, z1, z2):
    row = lax.broadcasted_iota(jnp.int32, (32, 128), 0)
    lane = lax.broadcasted_iota(jnp.int32, (32, 128), 1)
    valid = ((row >= 8) | (me > 0)) & ((row < 24) | (me < DEVICES - 1))
    for j in range(TILES):
        kappa[:, tile(j)] = jnp.where(valid, jnp.exp(lx[:, tile(j)]), 0.0)
    sums = [jnp.zeros((16, 128), F32) for _ in range(8)]
    for j, k, kn, ks, kw, ke in neighbours(lambda j: kappa[:, tile(j)]):
        north, south, west, east = 0.5 * (k + kn), 0.5 * (k + ks), 0.5 * (k + kw), 0.5 * (k + ke)
        d = north + south + west + east
        inverse = jnp.where(valid, 1.0 / d, 0.0)
        coefs[0, :, tile(j)] = north * inverse
        coefs[1, :, tile(j)] = south * inverse
        coefs[2, :, tile(j)] = west * inverse
        coefs[3, :, tile(j)] = east * inverse
        source = sx[:, tile(j)]
        first = source * inverse
        diag[:, tile(j)] = d[OWN]
        v0[:, tile(j)] = first
        sums[0] = sums[0] + source[OWN] * first[OWN]

    def beside(values):
        for j, v, vn, vs, vw, ve in neighbours(lambda j: values[:, tile(j)]):
            yield j, v, (coefs[0, :, tile(j)] * vn + coefs[1, :, tile(j)] * vs) + (
                coefs[2, :, tile(j)] * vw + coefs[3, :, tile(j)] * ve
            )

    for j, v, s in beside(v0):
        z = v - s
        z0[:, tile(j)] = z
        own = z[OWN]
        sums[1] = sums[1] + sx[OWN, tile(j)] * own
        sums[2] = sums[2] + diag[:, tile(j)] * own * own
    for j, v, s in beside(z0):
        z = -s
        z1[:, tile(j)] = z
        own = diag[:, tile(j)] * z[OWN]
        sums[3] = sums[3] + own * v[OWN]
        sums[4] = sums[4] + own * z[OWN]
    for j, v, s in beside(z1):
        z = -2.0 * s - z0[:, tile(j)]
        z2[:, tile(j)] = z
        own = diag[:, tile(j)] * z[OWN]
        sums[5] = sums[5] + own * v[OWN]
        sums[6] = sums[6] + own * z[OWN]
    for j, v, s in beside(z2):
        z = -2.0 * s[OWN] - z1[OWN, tile(j)]
        sums[7] = sums[7] + diag[:, tile(j)] * v[OWN] * z
    return sums


def lane_totals(sums):
    count = len(sums)
    high = -(-count // 8) * 8
    rows = [jnp.sum(s, axis=0, keepdims=True) for s in sums] + [jnp.zeros((1, 128), F32)] * (high - count)
    rows = jnp.concatenate(rows, axis=0)
    totals = jnp.broadcast_to(jnp.sum(rows, axis=1, keepdims=True), (high, 128))
    at = lax.broadcasted_iota(jnp.int32, (high, 128), 0) == lax.broadcasted_iota(jnp.int32, (high, 128), 1)
    return jnp.sum(jnp.where(at, totals, 0.0), axis=0, keepdims=True)


def share(me, row, mine, all_rows, sems):
    mine[0:1, :] = row
    all_rows[pl.ds(me, 1), :] = row
    send_to_all(me, lambda d: mine.at[pl.ds(0, 1), :], lambda s: all_rows.at[pl.ds(s, 1), :], sems.at[0], sems.at[1])


def shared(me, all_rows, sems):
    wait_for_all(me, all_rows.at[pl.ds(0, DEVICES - 1), :], sems.at[0], sems.at[1])


PAIRS = [(i, j) for i in range(4) for j in range(i, 4)]


def misfit_parts(guess, fields, counts, means, spread):
    sums = [spread[...]] + [jnp.zeros((8, 128), F32) for _ in range(14)]
    for j in range(TILES):
        for g in range(2):
            rows = slice(128 * g + 8 * j, 128 * g + 8 * j + 8)
            us = [f[8 + 8 * g : 16 + 8 * g, tile(j)] for f in fields]
            n = counts[rows, :128]
            off = ((guess[0] * us[0] + guess[1] * us[1]) + (guess[2] * us[2] + guess[3] * us[3])) - means[rows, :]
            many = n * off
            sums[0] = sums[0] + many * off
            for i in range(4):
                sums[1 + i] = sums[1 + i] + many * us[i]
            scaled_us = [n * u for u in us]
            for k, (i, l) in enumerate(PAIRS):
                sums[5 + k] = sums[5 + k] + scaled_us[i] * us[l]
    row = lane_totals(sums)
    lane = lax.broadcasted_iota(jnp.int32, (1, 128), 1)
    for i in range(4):
        row = jnp.where(lane == 15 + i, guess[i][:1], row)
    return pltpu.roll(jnp.broadcast_to(row, (8, 128)), 8, 1)[:1]


def misfit(y, rows):
    table = rows.T[8:]
    off = [y[i][:1] - table[15 + i : 16 + i] for i in range(4)]
    total = table[0:1]
    for i in range(4):
        total = total + 2.0 * off[i] * table[1 + i : 2 + i]
    for k, (i, l) in enumerate(PAIRS):
        term = off[i] * off[l] * table[5 + k : 6 + k]
        total = total + (term if i == l else 2.0 * term)
    return jnp.sum(total)


def weights(row):
    take = [jnp.broadcast_to(row[:, i : i + 1], (8, 128)) for i in range(8)]
    g0, e0, m0, m1, q11, q12, q22, q23 = take
    m2 = 2.0 * q11 - m0
    m3 = 2.0 * q12 - m1
    m4 = 2.0 * q22 - m0
    m5 = 2.0 * q23 - m1
    m = [m0, m1, m2, m3, m4, m5]

    def inner(i, j):
        return 0.5 * (m[i + j] + m[abs(i - j)])

    def energy(i, j):
        return inner(i, j) + 0.5 * (inner(i, j + 1) + inner(i, abs(j - 1)))

    gram = [[None] * 4 for _ in range(4)]
    gram[0][0] = e0
    for j in range(3):
        gram[j + 1][0] = inner(0, j)
        for i in range(j + 1):
            gram[j + 1][i + 1] = energy(i, j)
    right = [g0, e0, m0 - e0, 2.0 * (m1 - (m0 - e0)) - e0]
    factors = [[None] * 4 for _ in range(4)]
    inverse = []
    whole = [gram[i][i] for i in range(4)]
    for k in range(4):
        pivot = gram[k][k]
        inverse.append(jnp.where(pivot > 1e-6 * whole[k], 1.0 / pivot, 0.0))
        for i in range(k + 1, 4):
            factors[i][k] = gram[i][k] * inverse[k]
        for i in range(k + 1, 4):
            for j in range(k + 1, i + 1):
                gram[i][j] = gram[i][j] - factors[i][k] * gram[j][k]
            right[i] = right[i] - factors[i][k] * right[k]
    out = [right[k] * inverse[k] for k in range(4)]
    for k in (2, 1, 0):
        for i in range(k + 1, 4):
            out[k] = out[k] - factors[i][k] * out[i]
    return out


LOADS = ("state", "noise", "source", "cells", "values",
         "row_forward", "row_back", "row_turn", "col_forward", "col_back", "col_turn", "mid_forward", "mid_back")


def kernel(*refs):
    (step, sigma, wave), refs = refs[:3], refs[3:]
    count = len(LOADS)
    sources, refs = refs[:count], refs[count:]
    (log_perm_out, pressure_out, loglik), refs = refs[:3], refs[3:]
    held, refs = refs[:count], refs[count:]
    (
        z_high, z_low, sent1, got1, amp, sent2, got2,
        counts, means, hot, parts, spread,
        lx, sx, kappa, coefs, diag, v0, z0, z1, z2, mine, everyone, pressure, sems, load_sems, edge_sems, end_sems,
    ) = refs
    me = lax.axis_index(AXIS)
    loads = {
        name: pltpu.make_async_copy(sources[k], held[k], load_sems.at[k]) for k, name in enumerate(LOADS)
    }
    early = ("state", "noise", "row_turn", "row_forward")
    for name in early:
        loads[name].start()
    (state, noise, source, cells, values,
     row_forward, row_back, row_turn, col_forward, col_back, col_turn, mid_forward, mid_back) = held
    greet_all(me)
    for name in early:
        loads[name].wait()
    for name in LOADS:
        if name not in early:
            loads[name].start()
    rows_forward(step[0], state, noise, row_turn, z_high, z_low, row_forward, sent1)
    loads["source"].wait()
    meet_all()
    for part in range(PARTS):
        send_to_all(
            me, lambda d: sent1.at[pl.ds(8 * d + PIECE * part, PIECE), :],
            lambda s: got1.at[pl.ds(8 * s + PIECE * part, PIECE), :], sems.at[2 * part], sems.at[2 * part + 1],
        )
    source_edges = exchange_edges(me, source.at[pl.ds(0, 8), :], source.at[pl.ds(8, 8), :], sx, edge_sems)
    for copy in source_edges:
        copy.start()
    own = pl.ds(pl.multiple_of(8 * me, 8), 8)
    got1[own, :] = sent1[own, :]
    sx[OWN, :] = source[...]
    amplitudes(me, sigma[0], wave[0], amp)
    for name in ("col_forward", "col_back", "col_turn", "mid_forward", "mid_back", "row_back", "cells", "values"):
        loads[name].wait()
    gather_observations(me, cells, values, counts, means, hot, parts)
    for part in range(PARTS):
        wait_for_all(me, got1.at[pl.ds(0, PIECE * (DEVICES - 1)), :], sems.at[2 * part], sems.at[2 * part + 1])
        columns(part, got1, amp, col_forward, col_back, col_turn, mid_forward, mid_back, sent2)
        send_to_all(
            me, lambda d: sent2.at[pl.ds(8 * d + PIECE * part, PIECE), :],
            lambda s: got2.at[pl.ds(8 * s + PIECE * part, PIECE), :],
            sems.at[2 * (PARTS + part)], sems.at[2 * (PARTS + part) + 1],
        )
    got2[own, :] = sent2[own, :]
    spread_observations(me, cells, values, means, hot, spread)
    for part in range(PARTS):
        wait_for_all(
            me, got2.at[pl.ds(0, PIECE * (DEVICES - 1)), :], sems.at[2 * (PARTS + part)], sems.at[2 * (PARTS + part) + 1]
        )

    def put(row, at, value):
        lx[row : row + 8, at : at + 128] = value

    rows_back(got2, row_back, row_turn, put)
    write = pltpu.make_async_copy(lx.at[pl.ds(8, FIELD), :], log_perm_out, load_sems.at[count])
    write.start()
    for copy in source_edges:
        copy.wait()
    sums = krylov(me, lx, sx, kappa, coefs, diag, v0, z0, z1, z2)
    row = lane_totals(sums)
    fields = (v0, z0, z1, z2)
    guess = weights(row)
    fine = jnp.abs(guess[0]) < 64.0
    for i in range(1, 4):
        fine = fine & (jnp.abs(guess[i]) < 64.0)
    guess = [jnp.where(fine, g, 0.0) for g in guess]
    share(me, row + misfit_parts(guess, fields, counts, means, spread), mine, everyone, end_sems)
    shared(me, everyone, end_sems)
    y = weights(jnp.sum(everyone[...], axis=0, keepdims=True))
    for j in range(TILES):
        for g in range(2):
            us = [f[8 + 8 * g : 16 + 8 * g, tile(j)] for f in fields]
            pressure[8 * g : 8 * g + 8, tile(j)] = (y[0] * us[0] + y[1] * us[1]) + (y[2] * us[2] + y[3] * us[3])
    write_pressure = pltpu.make_async_copy(pressure, pressure_out, load_sems.at[count + 1])
    write_pressure.start()
    loglik[0, 0] = F32(-2.0 / 8192) * misfit(y, everyone[...])
    write.wait()
    write_pressure.wait()


def finish(log_perm, pressure, loglik, log_perm_out, pressure_out, loglik_out, sems):
    copies = [
        pltpu.make_async_copy(log_perm, log_perm_out, sems.at[0]),
        pltpu.make_async_copy(pressure, pressure_out, sems.at[1]),
    ]
    for copy in copies:
        copy.start()
    loglik_out[0, 0] = loglik[0, 0]
    for copy in copies:
        copy.wait()


def body(state, noise, step, field_scale, wave_scale, source, obs_cells, obs_values):
    anywhere = pl.BlockSpec(memory_space=pl.ANY)
    smem = pl.BlockSpec(memory_space=pltpu.SMEM)
    field = pltpu.VMEM((32, N), F32)
    own = pltpu.VMEM((FIELD, N), F32)
    arrays = [state, noise, source, obs_cells.reshape(64, 128), obs_values.reshape(64, 128)]
    arrays += [jnp.asarray(t) for t in tables()]
    log_perm, pressure, loglik = pl.pallas_call(
        kernel,
        out_shape=(
            jax.ShapeDtypeStruct((FIELD, N), F32),
            jax.ShapeDtypeStruct((FIELD, N), F32),
            jax.ShapeDtypeStruct((1, 1), F32),
        ),
        in_specs=[pl.BlockSpec(memory_space=pltpu.SMEM)] * 3 + [anywhere] * len(arrays),
        out_specs=(anywhere, anywhere, smem),
        scratch_shapes=[
            pltpu.VMEM(a.shape, a.dtype) for a in arrays
        ] + [
            pltpu.VMEM((512, 512), BF16),
            pltpu.VMEM((512, 512), BF16),
            pltpu.VMEM((1024, 128), F32),
            pltpu.VMEM((1024, 128), F32),
            pltpu.VMEM((8, KS, 128), F32),
            pltpu.VMEM((1024, 128), F32),
            pltpu.VMEM((1024, 128), F32),
            pltpu.VMEM((256, 512), F32),
            pltpu.VMEM((256, 128), F32),
            pltpu.VMEM((8, 256, 1024), BF16),
            pltpu.VMEM((512, 1024), BF16),
            pltpu.VMEM((8, 128), F32),
            field,
            field,
            field,
            pltpu.VMEM((4, 32, N), F32),
            own,
            field,
            field,
            field,
            field,
            pltpu.VMEM((8, 128), F32),
            pltpu.VMEM((DEVICES, 128), F32),
            own,
            pltpu.SemaphoreType.DMA((4 * PARTS,)),
            pltpu.SemaphoreType.DMA((len(arrays) + 2,)),
            pltpu.SemaphoreType.DMA((4,)),
            pltpu.SemaphoreType.DMA((2,)),
        ],
        compiler_params=pltpu.CompilerParams(collective_id=0, has_side_effects=True, vmem_limit_bytes=40 * 2**20),
    )(step, field_scale, wave_scale, *[pltpu.with_memory_space_constraint(a, pltpu.HBM) for a in arrays])
    log_perm, pressure, loglik = pl.pallas_call(
        finish,
        out_shape=(
            jax.ShapeDtypeStruct((FIELD, N), F32),
            jax.ShapeDtypeStruct((FIELD, N), F32),
            jax.ShapeDtypeStruct((1, 1), F32),
        ),
        in_specs=[anywhere, anywhere, smem],
        out_specs=(anywhere, anywhere, smem),
        scratch_shapes=[pltpu.SemaphoreType.DMA((2,))],
        compiler_params=pltpu.CompilerParams(vmem_limit_bytes=2**20),
    )(log_perm, pressure, loglik)
    return log_perm, pressure, loglik.reshape(())


def solution(mesh):
    in_specs = (P(AXIS, None), P(AXIS, None), P(), P(), P(), P(AXIS, None), P(), P())
    out_specs = (P(AXIS, None), P(AXIS, None), P())
    return jax.shard_map(body, mesh=mesh, in_specs=in_specs, out_specs=out_specs, check_vma=False)
```

```python
import functools
import math

import jax
import jax.numpy as jnp
import ml_dtypes
import numpy as np
from jax import lax
from jax.experimental import pallas as pl
from jax.experimental.pallas import tpu as pltpu
from jax.sharding import PartitionSpec as P

M = 4096
N = 2048
DEVICES = 128
ROWS = M // DEVICES
FIELD = N // DEVICES
KS = 72
ARRIVALS = ((0, 2), (2, 4))
DEPARTURES = ((0, 2), (2, 4))
AXIS = "strip"
MESH = pl.DeviceIdType.MESH
F32 = jnp.float32
BF16 = jnp.bfloat16


def halves(table):
    table = table.astype(np.float32)
    high = table.astype(ml_dtypes.bfloat16)
    low = (table - high.astype(np.float32)).astype(ml_dtypes.bfloat16)
    return np.stack([high, low])


def tables():
    b = np.arange(256)
    kl = np.arange(128)
    angle = 2 * np.pi * np.outer(kl, b) / 256
    top = np.zeros((16, 512))
    top[0, :256] = (-1.0) ** b
    row_forward = np.concatenate(
        [
            np.concatenate([np.cos(angle), np.sin(angle)], 1),
            np.concatenate([-np.sin(angle), np.cos(angle)], 1),
            top,
        ]
    )
    row_back = np.concatenate(
        [
            np.concatenate([np.cos(angle), np.sin(angle)], 1),
            np.concatenate([-np.sin(angle), np.cos(angle)], 1),
        ]
    )
    kv = np.arange(16)
    turn = 2 * np.pi * np.outer(kv, b) / M
    row_turn = np.stack([np.cos(turn), np.sin(turn)])
    ks = np.arange(KS)
    real = ks <= 64
    src = np.arange(DEVICES)
    angle = 2 * np.pi * np.outer(ks, src) / 128
    col_forward = np.concatenate([np.cos(angle), -np.sin(angle)]) * np.tile(real, 2)[:, None]
    weight = np.where((ks == 0) | (ks == 64), 1.0, 2.0) * real
    angle = angle.T[:64]
    col_back = np.concatenate([np.cos(angle) * weight, -np.sin(angle) * weight], 1)
    r = np.arange(32)
    lanes_in = [(v, q) for v in range(4) for q in range(32)]
    lanes_out = [(v, h * 8 + q) for h in range(4) for v in range(4) for q in range(8)]
    turn = 2 * np.pi * np.outer(ks, [q for _, q in lanes_in]) / M
    turn_back = 2 * np.pi * np.outer(ks, [q for _, q in lanes_out]) / M
    col_turn = np.stack([np.cos(turn), np.sin(turn), np.cos(turn_back), np.sin(turn_back)])
    vi, qi = np.array(lanes_in).T
    vo, qo = np.array(lanes_out).T
    same = vi[:, None] == vi[None, :]
    angle = 2 * np.pi * qi[:, None] * qi[None, :] / 32
    c, s = np.cos(angle) * same, np.sin(angle) * same
    mid_forward = np.block([[c, -s], [s, c]])
    same = vi[:, None] == vo[None, :]
    angle = 2 * np.pi * qi[:, None] * qo[None, :] / 32
    c, s = np.cos(angle) * same, np.sin(angle) * same
    mid_back = np.block([[c, s], [-s, c]])
    return (
        halves(row_forward),
        halves(row_back),
        row_turn.astype(np.float32),
        halves(col_forward),
        np.concatenate([halves(col_back)[k] for k in (0, 0, 1)], axis=1),
        col_turn.astype(np.float32),
        halves(mid_forward),
        halves(mid_back),
    )


def split(x):
    high = x.astype(BF16)
    return high, (x - high.astype(F32)).astype(BF16)


NN = (((1,), (0,)), ((), ()))
NT = (((1,), (1,)), ((), ()))


def product(left, right, form):
    (lh, ll), (rh, rl) = left, right
    axis_left, axis_right = form[0][0][0], form[0][1][0]
    return lax.dot_general(
        jnp.concatenate([lh, lh, ll], axis=axis_left),
        jnp.concatenate([rh, rl, rh], axis=axis_right),
        dimension_numbers=form,
        preferred_element_type=F32,
    )


def scaled(x, factor):
    if abs(factor) < 1e-12:
        return None
    if abs(factor - 1) < 1e-12:
        return x
    if abs(factor + 1) < 1e-12:
        return -x
    return x * F32(factor)


def plus(a, b):
    return b if a is None else a if b is None else a + b


def minus(a, b):
    if b is None:
        return a
    return -b if a is None else a - b


def turned(z, cos, sin):
    re, im = z
    out_re = scaled(re, cos) if re is not None else None
    out_im = scaled(re, sin) if re is not None else None
    if im is not None:
        out_re = minus(out_re, scaled(im, sin))
        out_im = plus(out_im, scaled(im, cos))
    return out_re, out_im


def added(a, b):
    return plus(a[0], b[0]), plus(a[1], b[1])


def less(a, b):
    return minus(a[0], b[0]), minus(a[1], b[1])


def real_dft(xs):
    count = len(xs)
    if count == 1:
        return [(xs[0], None)]
    even, odd = real_dft(xs[::2]), real_dft(xs[1::2])
    out = [None] * (count // 2 + 1)
    if count == 2:
        return [added(even[0], odd[0]), less(even[0], odd[0])]
    for k in range(count // 4 + 1):
        angle = -2 * math.pi * k / count
        t = turned(odd[k], math.cos(angle), math.sin(angle))
        out[k] = added(even[k], t)
        if k != count // 4:
            re, im = less(even[k], t)
            out[count // 2 - k] = (re, None if im is None else -im)
    return out


def back_dft(zs):
    count = len(zs)
    if count == 1:
        return list(zs)
    even, odd = back_dft(zs[::2]), back_dft(zs[1::2])
    out = [None] * count
    for k in range(count // 2):
        angle = 2 * math.pi * k / count
        t = turned(odd[k], math.cos(angle), math.sin(angle))
        out[k] = added(even[k], t)
        out[k + count // 2] = less(even[k], t)
    return out


def back_dft_real_first_half(zs):
    count = len(zs)
    even, odd = back_dft(zs[::2]), back_dft(zs[1::2])
    out = []
    for k in range(count // 2):
        angle = 2 * math.pi * k / count
        out.append(even[k][0] + turned(odd[k], math.cos(angle), math.sin(angle))[0])
    return out


def others_far_first(me):
    core, y, x, z = me % 2, (me // 2) % 4, (me // 8) % 4, me // 32
    cores = [core, 1 - core]
    ys = [2 * ((y + i) % 4) for i in range(4)]
    xs = [8 * ((x + i) % 4) for i in range(4)]
    zs = [32 * ((z + i) % 4) for i in range(4)]
    hops = (0, 1, 2, 1)
    offsets = [(a, b, c, d) for a in range(4) for b in range(4) for c in range(4) for d in range(2)][1:]
    offsets.sort(key=lambda o: (-(hops[o[0]] + hops[o[1]] + hops[o[2]]), (37 * o[0] + 17 * o[1] + 11 * o[2] + 5 * o[3]) % 13))
    return [(zs[a] + xs[b]) + (ys[c] + cores[d]) for a, b, c, d in offsets]


def send_to_all(me, others, piece, landing, send_sem, recv_sem):
    for other in others(me):
        pltpu.make_async_remote_copy(
            src_ref=piece(other),
            dst_ref=landing(me),
            send_sem=send_sem,
            recv_sem=recv_sem,
            device_id=(other,),
            device_id_type=MESH,
        ).start()


def wait_for_all(me, whole, send_sem, recv_sem):
    pltpu.make_async_remote_copy(
        src_ref=whole,
        dst_ref=whole,
        send_sem=send_sem,
        recv_sem=recv_sem,
        device_id=(lax.rem(me + 1, DEVICES),),
        device_id_type=MESH,
    ).wait()


def greet_all(me):
    barrier = pltpu.get_barrier_semaphore()

    for other in others_far_first(me):
        pl.semaphore_signal(barrier, inc=1, device_id=(other,), device_id_type=MESH)


def meet_all():
    pl.semaphore_wait(pltpu.get_barrier_semaphore(), DEVICES - 1)


def rows_forward(rate, state, noise, row_turn, z_high, z_low, row_forward, out):
    keep = jnp.sqrt(1.0 - rate * rate)
    for g in range(ROWS // 16):
        rows = slice(16 * g, 16 * g + 16)
        for h in range(2):
            xs = []
            for a in range(16):
                cols = slice(256 * a + 128 * h, 256 * a + 128 * h + 128)
                xs.append(keep * state[rows, cols] + rate * noise[rows, cols])
            ys = real_dft(xs)
            for kv in range(16):
                re, im = ys[kv] if kv <= 8 else ys[16 - kv]
                cos = row_turn[0, kv : kv + 1, 128 * h : 128 * h + 128]
                sin = row_turn[1, kv : kv + 1, 128 * h : 128 * h + 128]
                if kv > 8:
                    im = -im
                if kv == 0:
                    zr, zi = re, jnp.zeros_like(re)
                elif im is None:
                    zr, zi = re * cos, -(re * sin)
                else:
                    zr, zi = re * cos + im * sin, im * cos - re * sin
                spot = slice(kv * ROWS + 16 * g, kv * ROWS + 16 * g + 16)
                for part, lane in ((zr, 128 * h), (zi, 256 + 128 * h)):
                    high, low = split(part)
                    z_high[spot, lane : lane + 128] = high
                    z_low[spot, lane : lane + 128] = low
    for pair in range(2):
        rows = slice(256 * pair, 256 * pair + 256)
        res = product((row_forward[0], row_forward[1]), (z_high[rows, :], z_low[rows, :]), NT)
        for i in range(2):
            t = 2 * pair + i
            lanes = slice(128 * i, 128 * i + 128)
            im = res[128:256, lanes]
            if t == 0:
                first = (lax.broadcasted_iota(jnp.int32, (128, 128), 0) == 0) & (
                    lax.broadcasted_iota(jnp.int32, (128, 128), 1) < ROWS
                )
                im = jnp.where(first, jnp.broadcast_to(res[256:257, lanes], (128, 128)), im)
            out[pl.ds(t, 128, stride=8), :] = res[:128, lanes]
            out[pl.ds(4 + t, 128, stride=8), :] = im


def amplitudes(me, sigma, wave, amp):
    ks = lax.broadcasted_iota(jnp.int32, (KS, 128), 0)
    lane = lax.broadcasted_iota(jnp.int32, (KS, 128), 1)
    k0 = ks + 128 * (lane % 32)
    q0 = jnp.minimum(k0, M - k0).astype(F32)
    base = q0 * q0 + wave * wave
    gain = sigma * wave * F32(2.0 / (math.sqrt(math.pi) * M))
    for v in range(4):
        k1 = 16 * me + 4 * v + lane // 32
        q1 = k1.astype(F32)
        value = gain / (base + q1 * q1)
        if v == 0:
            alone = k1 == 0
            value = jnp.where(alone, 0.5 * value, value)
            top = jnp.where(alone, 0.5 * gain / (base + F32(N) * F32(N)), value)
            amp[4] = top
        else:
            amp[4 + v] = value
        amp[v] = value


def columns(first, last, got, amp, col_forward, col_back, col_turn, mid_forward, mid_back, out):
    tiles = list(range(2 * first, 2 * last))
    pieces = jnp.concatenate([got[pl.ds(t, 128, stride=8), :] for t in tiles], axis=1)
    spec = product((col_forward[0], col_forward[1]), split(pieces), NN)
    parts = []
    for i in range(len(tiles)):
        lanes = slice(128 * i, 128 * i + 128)
        re, im = spec[:KS, lanes], spec[KS:, lanes]
        cos, sin = col_turn[0], col_turn[1]
        parts.append(jnp.concatenate([re * cos + im * sin, im * cos - re * sin], axis=1))
    full = product(split(jnp.concatenate(parts, axis=0)), (mid_forward[0], mid_forward[1]), NN)
    factor = jnp.concatenate([amp[t] for t in tiles], axis=0)
    full = full * jnp.concatenate([factor, factor], axis=1)
    back = product(split(full), (mid_back[0], mid_back[1]), NN)
    sides = []
    for i in range(len(tiles)):
        rows = slice(KS * i, KS * i + KS)
        re, im = back[rows, :128], back[rows, 128:]
        cos, sin = col_turn[2], col_turn[3]
        sides.append(jnp.concatenate([re * cos - im * sin, im * cos + re * sin], axis=0))
    high, low = split(jnp.concatenate(sides, axis=1))
    field = lax.dot_general(col_back[...], jnp.concatenate([high, low, high], axis=0), NN, preferred_element_type=F32)
    lane = lax.broadcasted_iota(jnp.int32, (64, 128), 1)
    for i, t in enumerate(tiles):
        here = field[:, 128 * i : 128 * i + 128]
        later, sooner = pltpu.roll(here, 32, 1), pltpu.roll(here, 96, 1)
        out[pl.ds(t, 64, stride=16), :] = jnp.where(lane < 32, pltpu.roll(later, 1, 0), later)
        out[pl.ds(8 + t, 64, stride=16), :] = jnp.where(lane >= 96, pltpu.roll(sooner, 63, 0), sooner)


def rows_back(got, row_back, row_turn, put):
    blocks = [got[pl.ds(t, 128, stride=8), :].T for t in range(8)]
    row = lax.broadcasted_iota(jnp.int32, (128, 128), 0)
    lane = lax.broadcasted_iota(jnp.int32, (128, 128), 1)
    sign = (1 - 2 * (lane[:8] % 2)).astype(F32)
    tops = [jnp.broadcast_to(blocks[4][32 * g : 32 * g + 8, :1], (8, 128)) * sign for g in range(4)]
    blocks[4] = jnp.where((row % 32 < 8) & (lane == 0), 0.0, blocks[4])
    sides = jnp.concatenate([jnp.concatenate(blocks[:4], axis=0), jnp.concatenate(blocks[4:], axis=0)], axis=1)
    q = product(split(sides), (row_back[0], row_back[1]), NN)
    for h in range(2):
        for g in range(4):
            zs = []
            for kv in range(16):
                at = 128 * (kv // 4) + 32 * g + 8 * (kv % 4)
                rows = slice(at, at + 8)
                zr, zi = q[rows, 128 * h : 128 * h + 128], q[rows, 256 + 128 * h : 384 + 128 * h]
                cos = row_turn[0, kv : kv + 1, 128 * h : 128 * h + 128]
                sin = row_turn[1, kv : kv + 1, 128 * h : 128 * h + 128]
                zs.append((zr, zi) if kv == 0 else (zr * cos - zi * sin, zi * cos + zr * sin))
            for a, value in enumerate(back_dft_real_first_half(zs)):
                put(8 * g, 256 * a + 128 * h, value + tops[g])


def gather_observations(me, cells, values, counts, means, hot, parts):
    counts[...] = jnp.zeros_like(counts)

    @pl.loop(0, 8)
    def _(c):
        for i in range(8):
            cell = cells[pl.ds(8 * c + i, 1), :]
            value = values[pl.ds(8 * c + i, 1), :]
            row = cell // N - FIELD * me
            col = cell % N
            inside = (row >= 0) & (row < FIELD)
            spot = jnp.where(inside, (row // 8) * 128 + (col // 128) * 8 + row % 8, -1)
            lane = jnp.where(inside, col % 128, -1)
            lanes = slice(128 * i, 128 * i + 128)
            here = lax.broadcasted_iota(jnp.int32, (256, 128), 0) == spot
            hot[c, :, lanes] = jnp.where(here, 1.0, 0.0).astype(BF16)
            there = lax.broadcasted_iota(jnp.int32, (128, 128), 0) == lane
            high = value.astype(BF16).astype(F32)
            middle = (value - high).astype(BF16).astype(F32)
            low = value - high - middle
            for j, piece in enumerate((jnp.ones_like(value), high, middle, low)):
                parts[128 * j : 128 * j + 128, lanes] = jnp.where(there, piece, 0.0).astype(BF16)
        counts[...] += lax.dot_general(hot[c], parts[...], NT, preferred_element_type=F32)

    number = counts[:, :128]
    total = counts[:, 128:256] + counts[:, 256:384] + counts[:, 384:]
    means[...] = total / jnp.maximum(number, 1.0)


def spread_observations(me, cells, values, means, hot, spread):
    turned_means = jnp.concatenate([means[:128, :].T, means[128:, :].T], axis=1)
    pieces = jnp.concatenate(split(turned_means), axis=0)
    spread[...] = jnp.zeros_like(spread)

    @pl.loop(0, 8)
    def _(c):
        totals = [jnp.zeros((8, 128), F32) for _ in range(4)]
        for b in range(4):
            picked = jnp.dot(pieces, hot[c, :, 256 * b : 256 * b + 256], preferred_element_type=F32)
            for i in range(2):
                cell = cells[pl.ds(8 * c + 2 * b + i, 1), :]
                value = values[pl.ds(8 * c + 2 * b + i, 1), :]
                row = cell // N - FIELD * me
                lane = jnp.where((row >= 0) & (row < FIELD), cell % 128, -1)
                lanes = slice(128 * i, 128 * i + 128)
                mean = picked[:128, lanes] + picked[128:, lanes]
                there = lax.broadcasted_iota(jnp.int32, (128, 128), 0) == lane
                off = jnp.where(there, value - mean, 0.0)
                off = off * off
                for k in range(16):
                    totals[k % 4] = totals[k % 4] + off[8 * k : 8 * k + 8]
        spread[...] += (totals[0] + totals[1]) + (totals[2] + totals[3])


def exchange_edges(me, own_low, own_high, ext, sems):
    up, down = lax.rem(me + 1, DEVICES), lax.rem(me + DEVICES - 1, DEVICES)
    return [
        pltpu.make_async_remote_copy(
            src_ref=own_low, dst_ref=ext.at[pl.ds(24, 8), :], send_sem=sems.at[0], recv_sem=sems.at[1],
            device_id=(down,), device_id_type=MESH,
        ),
        pltpu.make_async_remote_copy(
            src_ref=own_high, dst_ref=ext.at[pl.ds(0, 8), :], send_sem=sems.at[2], recv_sem=sems.at[3],
            device_id=(up,), device_id_type=MESH,
        ),
    ]


TILES = N // 128
OWN = slice(8, 24)


def tile(j):
    return slice(128 * j, 128 * j + 128)


def neighbours(load):
    lane = lax.broadcasted_iota(jnp.int32, (32, 128), 1)
    values = [load(0), load(1)]
    rights = [pltpu.roll(v, 1, 1) for v in values]
    lefts = [pltpu.roll(v, 127, 1) for v in values]
    before = jnp.zeros_like(rights[0])
    for j in range(TILES):
        if j == TILES - 1:
            after = jnp.zeros_like(before)
        else:
            after = lefts[1]
        west = jnp.where(lane == 0, before, rights[0])
        east = jnp.where(lane == 127, after, lefts[0])
        north = pltpu.roll(values[0], 1, 0)
        south = pltpu.roll(values[0], 31, 0)
        yield j, values[0], north, south, west, east
        before = rights[0]
        if j + 1 < TILES:
            values = values[1:]
            rights = rights[1:]
            lefts = lefts[1:]
            if j + 2 < TILES:
                values.append(load(j + 2))
                rights.append(pltpu.roll(values[1], 1, 1))
                lefts.append(pltpu.roll(values[1], 127, 1))


def krylov(me, lx, sx, kappa, coefs, diag, v0, z0, z1, z2):
    row = lax.broadcasted_iota(jnp.int32, (32, 128), 0)
    lane = lax.broadcasted_iota(jnp.int32, (32, 128), 1)
    valid = ((row >= 8) | (me > 0)) & ((row < 24) | (me < DEVICES - 1))
    for j in range(TILES):
        kappa[:, tile(j)] = jnp.where(valid, jnp.exp(lx[:, tile(j)]), 0.0)
    sums = [jnp.zeros((16, 128), F32) for _ in range(8)]
    for j, k, kn, ks, kw, ke in neighbours(lambda j: kappa[:, tile(j)]):
        north, south, west, east = 0.5 * (k + kn), 0.5 * (k + ks), 0.5 * (k + kw), 0.5 * (k + ke)
        d = north + south + west + east
        inverse = jnp.where(valid, 1.0 / d, 0.0)
        coefs[0, :, tile(j)] = north * inverse
        coefs[1, :, tile(j)] = south * inverse
        coefs[2, :, tile(j)] = west * inverse
        coefs[3, :, tile(j)] = east * inverse
        source = sx[:, tile(j)]
        first = source * inverse
        diag[:, tile(j)] = d[OWN]
        v0[:, tile(j)] = first
        sums[0] = sums[0] + source[OWN] * first[OWN]

    def beside(values):
        for j, v, vn, vs, vw, ve in neighbours(lambda j: values[:, tile(j)]):
            yield j, v, (coefs[0, :, tile(j)] * vn + coefs[1, :, tile(j)] * vs) + (
                coefs[2, :, tile(j)] * vw + coefs[3, :, tile(j)] * ve
            )

    for j, v, s in beside(v0):
        z = v - s
        z0[:, tile(j)] = z
        own = z[OWN]
        sums[1] = sums[1] + sx[OWN, tile(j)] * own
        sums[2] = sums[2] + diag[:, tile(j)] * own * own
    for j, v, s in beside(z0):
        z = -s
        z1[:, tile(j)] = z
        own = diag[:, tile(j)] * z[OWN]
        sums[3] = sums[3] + own * v[OWN]
        sums[4] = sums[4] + own * z[OWN]
    for j, v, s in beside(z1):
        z = -2.0 * s - z0[:, tile(j)]
        z2[:, tile(j)] = z
        own = diag[:, tile(j)] * z[OWN]
        sums[5] = sums[5] + own * v[OWN]
        sums[6] = sums[6] + own * z[OWN]
    for j, v, s in beside(z2):
        z = -2.0 * s[OWN] - z1[OWN, tile(j)]
        sums[7] = sums[7] + diag[:, tile(j)] * v[OWN] * z
    return sums


def lane_totals(sums):
    count = len(sums)
    high = -(-count // 8) * 8
    rows = [jnp.sum(s, axis=0, keepdims=True) for s in sums] + [jnp.zeros((1, 128), F32)] * (high - count)
    rows = jnp.concatenate(rows, axis=0)
    totals = jnp.broadcast_to(jnp.sum(rows, axis=1, keepdims=True), (high, 128))
    at = lax.broadcasted_iota(jnp.int32, (high, 128), 0) == lax.broadcasted_iota(jnp.int32, (high, 128), 1)
    return jnp.sum(jnp.where(at, totals, 0.0), axis=0, keepdims=True)


def share(me, row, mine, all_rows, sems):
    mine[0:1, :] = row
    all_rows[pl.ds(me, 1), :] = row
    send_to_all(me, others_far_first, lambda d: mine.at[pl.ds(0, 1), :], lambda s: all_rows.at[pl.ds(s, 1), :], sems.at[0], sems.at[1])


def shared(me, all_rows, sems):
    wait_for_all(me, all_rows.at[pl.ds(0, DEVICES - 1), :], sems.at[0], sems.at[1])


PAIRS = [(i, j) for i in range(4) for j in range(i, 4)]


def misfit_parts(guess, fields, counts, means, spread):
    sums = [spread[...]] + [jnp.zeros((8, 128), F32) for _ in range(14)]
    for j in range(TILES):
        for g in range(2):
            rows = slice(128 * g + 8 * j, 128 * g + 8 * j + 8)
            us = [f[8 + 8 * g : 16 + 8 * g, tile(j)] for f in fields]
            n = counts[rows, :128]
            off = ((guess[0] * us[0] + guess[1] * us[1]) + (guess[2] * us[2] + guess[3] * us[3])) - means[rows, :]
            many = n * off
            sums[0] = sums[0] + many * off
            for i in range(4):
                sums[1 + i] = sums[1 + i] + many * us[i]
            scaled_us = [n * u for u in us]
            for k, (i, l) in enumerate(PAIRS):
                sums[5 + k] = sums[5 + k] + scaled_us[i] * us[l]
    row = lane_totals(sums)
    lane = lax.broadcasted_iota(jnp.int32, (1, 128), 1)
    for i in range(4):
        row = jnp.where(lane == 15 + i, guess[i][:1], row)
    return pltpu.roll(jnp.broadcast_to(row, (8, 128)), 8, 1)[:1]


def misfit(y, rows):
    table = rows.T[8:]
    off = [y[i][:1] - table[15 + i : 16 + i] for i in range(4)]
    total = table[0:1]
    for i in range(4):
        total = total + 2.0 * off[i] * table[1 + i : 2 + i]
    for k, (i, l) in enumerate(PAIRS):
        term = off[i] * off[l] * table[5 + k : 6 + k]
        total = total + (term if i == l else 2.0 * term)
    return jnp.sum(total)


def pair_sum(x, y):
    total = x[0] + y[0]
    step = total - x[0]
    rest = (x[0] - (total - step)) + (y[0] - step)
    rest = rest + (x[1] + y[1])
    high = total + rest
    return high, rest - (high - total)


def pair_scaled(x, factor):
    return x[0] * F32(factor), x[1] * F32(factor)


def pair_total(rows):
    zero = jnp.zeros((8, 128), F32)
    terms = [(rows[8 * k : 8 * k + 8], zero) for k in range(DEVICES // 8)]
    while len(terms) > 1:
        terms = [pair_sum(terms[2 * k], terms[2 * k + 1]) for k in range(len(terms) // 2)]
    total = terms[0]
    for shift in (4, 2, 1):
        total = pair_sum(total, (pltpu.roll(total[0], shift, 0), pltpu.roll(total[1], shift, 0)))
    return total


def cut(a):
    t = F32(4097.0) * a
    high = t - (t - a)
    return high, a - high


def system(take, scale, add):
    g0, e0, m0, m1, q11, q12, q22, q23 = take

    def less(a, b):
        return add(a, scale(b, -1.0))

    m = [m0, m1, less(scale(q11, 2.0), m0), less(scale(q12, 2.0), m1), less(scale(q22, 2.0), m0), less(scale(q23, 2.0), m1)]

    def inner(i, j):
        return scale(add(m[i + j], m[abs(i - j)]), 0.5)

    def energy(i, j):
        return add(inner(i, j), scale(add(inner(i, j + 1), inner(i, abs(j - 1))), 0.5))

    gram = [[None] * 4 for _ in range(4)]
    gram[0][0] = e0
    for j in range(3):
        gram[j + 1][0] = inner(0, j)
        for i in range(j + 1):
            gram[j + 1][i + 1] = energy(i, j)
    tail = less(m0, e0)
    return gram, [g0, e0, tail, less(scale(less(m1, tail), 2.0), e0)]


def lanes_of(row):
    return [jnp.broadcast_to(row[:1, i : i + 1], (8, 128)) for i in range(8)]


def solver(gram):
    gram = [list(r) for r in gram]
    factors = [[None] * 4 for _ in range(4)]
    inverse = []
    whole = [gram[i][i] for i in range(4)]
    for k in range(4):
        pivot = gram[k][k]
        inverse.append(jnp.where(pivot > 1e-6 * whole[k], 1.0 / pivot, 0.0))
        for i in range(k + 1, 4):
            factors[i][k] = gram[i][k] * inverse[k]
        for i in range(k + 1, 4):
            for j in range(k + 1, i + 1):
                gram[i][j] = gram[i][j] - factors[i][k] * gram[j][k]

    def solve(right):
        right = list(right)
        for k in range(4):
            for i in range(k + 1, 4):
                right[i] = right[i] - factors[i][k] * right[k]
        out = [right[k] * inverse[k] for k in range(4)]
        for k in (2, 1, 0):
            for i in range(k + 1, 4):
                out[k] = out[k] - factors[i][k] * out[i]
        return out

    return solve


def weights(row):
    gram, right = system(lanes_of(row), lambda a, f: a * F32(f), lambda a, b: a + b)
    return solver(gram)(right)


def refined_weights(total):
    gram, right = system(list(zip(lanes_of(total[0]), lanes_of(total[1]))), pair_scaled, pair_sum)
    solve = solver([[g and g[0] for g in r] for r in gram])
    y = solve([r[0] for r in right])
    y_cut = [cut(v) for v in y]
    cuts = [[g and cut(g[0]) for g in r] for r in gram]
    left = []
    for i in range(4):
        rest = right[i]
        for j in range(4):
            a, b = max(i, j), min(i, j)
            high, low = gram[a][b]
            (gh, gl), (yh, yl) = cuts[a][b], y_cut[j]
            main = high * y[j]
            error = ((gh * yh - main) + (gh * yl + gl * yh)) + gl * yl
            rest = pair_sum(rest, (-main, -(error + low * y[j])))
        left.append(rest[0] + rest[1])
    better = [v + d for v, d in zip(y, solve(left))]
    size = jnp.maximum(jnp.maximum(jnp.abs(y[0]), jnp.abs(y[1])), jnp.maximum(jnp.abs(y[2]), jnp.abs(y[3])))
    close = jnp.abs(better[0] - y[0]) <= 0.01 * size
    for k in range(1, 4):
        close = close & (jnp.abs(better[k] - y[k]) <= 0.01 * size)
    return [jnp.where(close, b, v) for b, v in zip(better, y)]


LOADS = ("state", "noise", "source", "cells", "values",
         "row_forward", "row_back", "row_turn", "col_forward", "col_back", "col_turn", "mid_forward", "mid_back")


def kernel(*refs):
    (step, sigma, wave), refs = refs[:3], refs[3:]
    count = len(LOADS)
    sources, refs = refs[:count], refs[count:]
    (log_perm_out, pressure_out, loglik), refs = refs[:3], refs[3:]
    held, refs = refs[:count], refs[count:]
    (
        z_high, z_low, sent1, got1, amp, sent2, got2,
        counts, means, hot, parts, spread,
        lx, sx, kappa, coefs, diag, v0, z0, z1, z2, mine, everyone, pressure, sems, load_sems, edge_sems, end_sems,
    ) = refs
    me = lax.axis_index(AXIS)
    loads = {
        name: pltpu.make_async_copy(sources[k], held[k], load_sems.at[k]) for k, name in enumerate(LOADS)
    }
    early = ("state", "noise", "row_turn", "row_forward")
    for name in early:
        loads[name].start()
    (state, noise, source, cells, values,
     row_forward, row_back, row_turn, col_forward, col_back, col_turn, mid_forward, mid_back) = held
    greet_all(me)
    for name in early:
        loads[name].wait()
    for name in LOADS:
        if name not in early:
            loads[name].start()
    rows_forward(step[0], state, noise, row_turn, z_high, z_low, row_forward, sent1)
    loads["source"].wait()
    meet_all()
    for part, (first, last) in enumerate(ARRIVALS):
        size = 2 * (last - first)
        send_to_all(
            me, others_far_first, lambda d: sent1.at[pl.ds(8 * d + 2 * first, size), :],
            lambda s: got1.at[pl.ds(8 * s + 2 * first, size), :], sems.at[2 * part], sems.at[2 * part + 1],
        )
    source_edges = exchange_edges(me, source.at[pl.ds(0, 8), :], source.at[pl.ds(8, 8), :], sx, edge_sems)
    for copy in source_edges:
        copy.start()
    own = pl.ds(pl.multiple_of(8 * me, 8), 8)
    got1[own, :] = sent1[own, :]
    sx[OWN, :] = source[...]
    amplitudes(me, sigma[0], wave[0], amp)
    for name in ("col_forward", "col_back", "col_turn", "mid_forward", "mid_back", "row_back", "cells", "values"):
        loads[name].wait()
    gather_observations(me, cells, values, counts, means, hot, parts)
    ready = 0
    for part, (first, last) in enumerate(DEPARTURES):
        while ready < len(ARRIVALS) and ARRIVALS[ready][0] < last:
            size = 2 * (ARRIVALS[ready][1] - ARRIVALS[ready][0])
            wait_for_all(me, got1.at[pl.ds(0, size * (DEVICES - 1)), :], sems.at[2 * ready], sems.at[2 * ready + 1])
            ready += 1
        columns(first, last, got1, amp, col_forward, col_back, col_turn, mid_forward, mid_back, sent2)
        size = 2 * (last - first)
        send_to_all(
            me, others_far_first, lambda d: sent2.at[pl.ds(8 * d + 2 * first, size), :],
            lambda s: got2.at[pl.ds(8 * s + 2 * first, size), :], sems.at[8 + 2 * part], sems.at[9 + 2 * part],
        )
    got2[own, :] = sent2[own, :]
    spread_observations(me, cells, values, means, hot, spread)
    for part, (first, last) in enumerate(DEPARTURES):
        size = 2 * (last - first)
        wait_for_all(me, got2.at[pl.ds(0, size * (DEVICES - 1)), :], sems.at[8 + 2 * part], sems.at[9 + 2 * part])

    def put(row, at, value):
        lx[row : row + 8, at : at + 128] = value

    rows_back(got2, row_back, row_turn, put)
    write = pltpu.make_async_copy(lx.at[pl.ds(8, FIELD), :], log_perm_out, load_sems.at[count])
    write.start()
    for copy in source_edges:
        copy.wait()
    sums = krylov(me, lx, sx, kappa, coefs, diag, v0, z0, z1, z2)
    row = lane_totals(sums)
    fields = (v0, z0, z1, z2)
    guess = weights(row)
    fine = jnp.abs(guess[0]) < 64.0
    for i in range(1, 4):
        fine = fine & (jnp.abs(guess[i]) < 64.0)
    guess = [jnp.where(fine, g, 0.0) for g in guess]
    share(me, row + misfit_parts(guess, fields, counts, means, spread), mine, everyone, end_sems)
    shared(me, everyone, end_sems)
    y = refined_weights(pair_total(everyone[...]))
    for j in range(TILES):
        for g in range(2):
            us = [f[8 + 8 * g : 16 + 8 * g, tile(j)] for f in fields]
            pressure[8 * g : 8 * g + 8, tile(j)] = (y[0] * us[0] + y[1] * us[1]) + (y[2] * us[2] + y[3] * us[3])
    write_pressure = pltpu.make_async_copy(pressure, pressure_out, load_sems.at[count + 1])
    write_pressure.start()
    loglik[0, 0] = F32(-2.0 / 8192) * misfit(y, everyone[...])
    write.wait()
    write_pressure.wait()


def finish(log_perm, pressure, loglik, log_perm_out, pressure_out, loglik_out, sems):
    copies = [
        pltpu.make_async_copy(log_perm, log_perm_out, sems.at[0]),
        pltpu.make_async_copy(pressure, pressure_out, sems.at[1]),
    ]
    for copy in copies:
        copy.start()
    loglik_out[0, 0] = loglik[0, 0]
    for copy in copies:
        copy.wait()


def body(state, noise, step, field_scale, wave_scale, source, obs_cells, obs_values):
    anywhere = pl.BlockSpec(memory_space=pl.ANY)
    smem = pl.BlockSpec(memory_space=pltpu.SMEM)
    field = pltpu.VMEM((32, N), F32)
    own = pltpu.VMEM((FIELD, N), F32)
    arrays = [state, noise, source, obs_cells.reshape(64, 128), obs_values.reshape(64, 128)]
    arrays += [jnp.asarray(t) for t in tables()]
    log_perm, pressure, loglik = pl.pallas_call(
        kernel,
        out_shape=(
            jax.ShapeDtypeStruct((FIELD, N), F32),
            jax.ShapeDtypeStruct((FIELD, N), F32),
            jax.ShapeDtypeStruct((1, 1), F32),
        ),
        in_specs=[pl.BlockSpec(memory_space=pltpu.SMEM)] * 3 + [anywhere] * len(arrays),
        out_specs=(anywhere, anywhere, smem),
        scratch_shapes=[
            pltpu.VMEM(a.shape, a.dtype) for a in arrays
        ] + [
            pltpu.VMEM((512, 512), BF16),
            pltpu.VMEM((512, 512), BF16),
            pltpu.VMEM((1024, 128), F32),
            pltpu.VMEM((1024, 128), F32),
            pltpu.VMEM((8, KS, 128), F32),
            pltpu.VMEM((1024, 128), F32),
            pltpu.VMEM((1024, 128), F32),
            pltpu.VMEM((256, 512), F32),
            pltpu.VMEM((256, 128), F32),
            pltpu.VMEM((8, 256, 1024), BF16),
            pltpu.VMEM((512, 1024), BF16),
            pltpu.VMEM((8, 128), F32),
            field,
            field,
            field,
            pltpu.VMEM((4, 32, N), F32),
            own,
            field,
            field,
            field,
            field,
            pltpu.VMEM((8, 128), F32),
            pltpu.VMEM((DEVICES, 128), F32),
            own,
            pltpu.SemaphoreType.DMA((16,)),
            pltpu.SemaphoreType.DMA((len(arrays) + 2,)),
            pltpu.SemaphoreType.DMA((4,)),
            pltpu.SemaphoreType.DMA((2,)),
        ],
        compiler_params=pltpu.CompilerParams(collective_id=0, has_side_effects=True, vmem_limit_bytes=40 * 2**20),
    )(step, field_scale, wave_scale, *[pltpu.with_memory_space_constraint(a, pltpu.HBM) for a in arrays])
    log_perm, pressure, loglik = pl.pallas_call(
        finish,
        out_shape=(
            jax.ShapeDtypeStruct((FIELD, N), F32),
            jax.ShapeDtypeStruct((FIELD, N), F32),
            jax.ShapeDtypeStruct((1, 1), F32),
        ),
        in_specs=[anywhere, anywhere, smem],
        out_specs=(anywhere, anywhere, smem),
        scratch_shapes=[pltpu.SemaphoreType.DMA((2,))],
        compiler_params=pltpu.CompilerParams(vmem_limit_bytes=2**20),
    )(log_perm, pressure, loglik)
    return log_perm, pressure, loglik.reshape(())


def solution(mesh):
    in_specs = (P(AXIS, None), P(AXIS, None), P(), P(), P(), P(AXIS, None), P(), P())
    out_specs = (P(AXIS, None), P(AXIS, None), P())
    return jax.shard_map(body, mesh=mesh, in_specs=in_specs, out_specs=out_specs, check_vma=False)
```

```python
import functools
import math

import jax
import jax.numpy as jnp
import ml_dtypes
import numpy as np
from jax import lax
from jax.experimental import pallas as pl
from jax.experimental.pallas import tpu as pltpu
from jax.sharding import PartitionSpec as P

M = 4096
N = 2048
DEVICES = 128
ROWS = M // DEVICES
FIELD = N // DEVICES
KS = 72
ARRIVALS = ((0, 2), (2, 4))
DEPARTURES = ((0, 2), (2, 4))
AXIS = "strip"
MESH = pl.DeviceIdType.MESH
F32 = jnp.float32
BF16 = jnp.bfloat16


def halves(table):
    table = table.astype(np.float32)
    high = table.astype(ml_dtypes.bfloat16)
    low = (table - high.astype(np.float32)).astype(ml_dtypes.bfloat16)
    return np.stack([high, low])


def tables():
    b = np.arange(256)
    kl = np.arange(128)
    angle = 2 * np.pi * np.outer(kl, b) / 256
    top = np.zeros((16, 512))
    top[0, :256] = (-1.0) ** b
    row_forward = np.concatenate(
        [
            np.concatenate([np.cos(angle), np.sin(angle)], 1),
            np.concatenate([-np.sin(angle), np.cos(angle)], 1),
            top,
        ]
    )
    row_back = np.concatenate(
        [
            np.concatenate([np.cos(angle), np.sin(angle)], 1),
            np.concatenate([-np.sin(angle), np.cos(angle)], 1),
        ]
    )
    kv = np.arange(16)
    turn = 2 * np.pi * np.outer(kv, b) / M
    row_turn = np.stack([np.cos(turn), np.sin(turn)])
    ks = np.arange(KS)
    real = ks <= 64
    src = np.arange(DEVICES)
    angle = 2 * np.pi * np.outer(ks, src) / 128
    col_forward = np.concatenate([np.cos(angle), -np.sin(angle)]) * np.tile(real, 2)[:, None]
    weight = np.where((ks == 0) | (ks == 64), 1.0, 2.0) * real
    angle = angle.T[:64]
    col_back = np.concatenate([np.cos(angle) * weight, -np.sin(angle) * weight], 1)
    r = np.arange(32)
    lanes_in = [(v, q) for v in range(4) for q in range(32)]
    lanes_out = [(v, h * 8 + q) for h in range(4) for v in range(4) for q in range(8)]
    turn = 2 * np.pi * np.outer(ks, [q for _, q in lanes_in]) / M
    turn_back = 2 * np.pi * np.outer(ks, [q for _, q in lanes_out]) / M
    col_turn = np.stack([np.cos(turn), np.sin(turn), np.cos(turn_back), np.sin(turn_back)])
    vi, qi = np.array(lanes_in).T
    vo, qo = np.array(lanes_out).T
    same = vi[:, None] == vi[None, :]
    angle = 2 * np.pi * qi[:, None] * qi[None, :] / 32
    c, s = np.cos(angle) * same, np.sin(angle) * same
    mid_forward = np.block([[c, -s], [s, c]])
    same = vi[:, None] == vo[None, :]
    angle = 2 * np.pi * qi[:, None] * qo[None, :] / 32
    c, s = np.cos(angle) * same, np.sin(angle) * same
    mid_back = np.block([[c, s], [-s, c]])
    return (
        halves(row_forward),
        halves(row_back),
        row_turn.astype(np.float32),
        halves(col_forward),
        np.concatenate([halves(col_back)[k] for k in (0, 0, 1)], axis=1),
        col_turn.astype(np.float32),
        halves(mid_forward),
        halves(mid_back),
    )


def split(x):
    high = x.astype(BF16)
    return high, (x - high.astype(F32)).astype(BF16)


NN = (((1,), (0,)), ((), ()))
NT = (((1,), (1,)), ((), ()))


def product(left, right, form):
    (lh, ll), (rh, rl) = left, right
    axis_left, axis_right = form[0][0][0], form[0][1][0]
    return lax.dot_general(
        jnp.concatenate([lh, lh, ll], axis=axis_left),
        jnp.concatenate([rh, rl, rh], axis=axis_right),
        dimension_numbers=form,
        preferred_element_type=F32,
    )


def scaled(x, factor):
    if abs(factor) < 1e-12:
        return None
    if abs(factor - 1) < 1e-12:
        return x
    if abs(factor + 1) < 1e-12:
        return -x
    return x * F32(factor)


def plus(a, b):
    return b if a is None else a if b is None else a + b


def minus(a, b):
    if b is None:
        return a
    return -b if a is None else a - b


def turned(z, cos, sin):
    re, im = z
    out_re = scaled(re, cos) if re is not None else None
    out_im = scaled(re, sin) if re is not None else None
    if im is not None:
        out_re = minus(out_re, scaled(im, sin))
        out_im = plus(out_im, scaled(im, cos))
    return out_re, out_im


def added(a, b):
    return plus(a[0], b[0]), plus(a[1], b[1])


def less(a, b):
    return minus(a[0], b[0]), minus(a[1], b[1])


def real_dft(xs):
    count = len(xs)
    if count == 1:
        return [(xs[0], None)]
    even, odd = real_dft(xs[::2]), real_dft(xs[1::2])
    out = [None] * (count // 2 + 1)
    if count == 2:
        return [added(even[0], odd[0]), less(even[0], odd[0])]
    for k in range(count // 4 + 1):
        angle = -2 * math.pi * k / count
        t = turned(odd[k], math.cos(angle), math.sin(angle))
        out[k] = added(even[k], t)
        if k != count // 4:
            re, im = less(even[k], t)
            out[count // 2 - k] = (re, None if im is None else -im)
    return out


def back_dft(zs):
    count = len(zs)
    if count == 1:
        return list(zs)
    even, odd = back_dft(zs[::2]), back_dft(zs[1::2])
    out = [None] * count
    for k in range(count // 2):
        angle = 2 * math.pi * k / count
        t = turned(odd[k], math.cos(angle), math.sin(angle))
        out[k] = added(even[k], t)
        out[k + count // 2] = less(even[k], t)
    return out


def back_dft_real_first_half(zs):
    count = len(zs)
    even, odd = back_dft(zs[::2]), back_dft(zs[1::2])
    out = []
    for k in range(count // 2):
        angle = 2 * math.pi * k / count
        out.append(even[k][0] + turned(odd[k], math.cos(angle), math.sin(angle))[0])
    return out


def others_far_first(me):
    core, y, x, z = me % 2, (me // 2) % 4, (me // 8) % 4, me // 32
    cores = [core, 1 - core]
    ys = [2 * ((y + i) % 4) for i in range(4)]
    xs = [8 * ((x + i) % 4) for i in range(4)]
    zs = [32 * ((z + i) % 4) for i in range(4)]
    hops = (0, 1, 2, 1)
    offsets = [(a, b, c, d) for a in range(4) for b in range(4) for c in range(4) for d in range(2)][1:]
    offsets.sort(key=lambda o: (-(hops[o[0]] + hops[o[1]] + hops[o[2]]), (37 * o[0] + 17 * o[1] + 11 * o[2] + 5 * o[3]) % 13))
    return [(zs[a] + xs[b]) + (ys[c] + cores[d]) for a, b, c, d in offsets]


def send_to_all(me, others, piece, landing, send_sem, recv_sem):
    for other in others(me):
        pltpu.make_async_remote_copy(
            src_ref=piece(other),
            dst_ref=landing(me),
            send_sem=send_sem,
            recv_sem=recv_sem,
            device_id=(other,),
            device_id_type=MESH,
        ).start()


def wait_for_all(me, whole, send_sem, recv_sem):
    pltpu.make_async_remote_copy(
        src_ref=whole,
        dst_ref=whole,
        send_sem=send_sem,
        recv_sem=recv_sem,
        device_id=(lax.rem(me + 1, DEVICES),),
        device_id_type=MESH,
    ).wait()


def greet_all(me):
    barrier = pltpu.get_barrier_semaphore()

    for other in others_far_first(me):
        pl.semaphore_signal(barrier, inc=1, device_id=(other,), device_id_type=MESH)


def meet_all():
    pl.semaphore_wait(pltpu.get_barrier_semaphore(), DEVICES - 1)


def rows_forward(rate, state, noise, row_turn, z_high, z_low, row_forward, out):
    keep = jnp.sqrt(1.0 - rate * rate)
    for g in range(ROWS // 16):
        rows = slice(16 * g, 16 * g + 16)
        for h in range(2):
            xs = []
            for a in range(16):
                cols = slice(256 * a + 128 * h, 256 * a + 128 * h + 128)
                xs.append(keep * state[rows, cols] + rate * noise[rows, cols])
            ys = real_dft(xs)
            for kv in range(16):
                re, im = ys[kv] if kv <= 8 else ys[16 - kv]
                cos = row_turn[0, kv : kv + 1, 128 * h : 128 * h + 128]
                sin = row_turn[1, kv : kv + 1, 128 * h : 128 * h + 128]
                if kv > 8:
                    im = -im
                if kv == 0:
                    zr, zi = re, jnp.zeros_like(re)
                elif im is None:
                    zr, zi = re * cos, -(re * sin)
                else:
                    zr, zi = re * cos + im * sin, im * cos - re * sin
                spot = slice(kv * ROWS + 16 * g, kv * ROWS + 16 * g + 16)
                for part, lane in ((zr, 128 * h), (zi, 256 + 128 * h)):
                    high, low = split(part)
                    z_high[spot, lane : lane + 128] = high
                    z_low[spot, lane : lane + 128] = low
    for pair in range(2):
        rows = slice(256 * pair, 256 * pair + 256)
        res = product((row_forward[0], row_forward[1]), (z_high[rows, :], z_low[rows, :]), NT)
        for i in range(2):
            t = 2 * pair + i
            lanes = slice(128 * i, 128 * i + 128)
            im = res[128:256, lanes]
            if t == 0:
                first = (lax.broadcasted_iota(jnp.int32, (128, 128), 0) == 0) & (
                    lax.broadcasted_iota(jnp.int32, (128, 128), 1) < ROWS
                )
                im = jnp.where(first, jnp.broadcast_to(res[256:257, lanes], (128, 128)), im)
            out[pl.ds(t, 128, stride=8), :] = res[:128, lanes]
            out[pl.ds(4 + t, 128, stride=8), :] = im


def amplitudes(me, sigma, wave, amp):
    ks = lax.broadcasted_iota(jnp.int32, (KS, 128), 0)
    lane = lax.broadcasted_iota(jnp.int32, (KS, 128), 1)
    k0 = ks + 128 * (lane % 32)
    q0 = jnp.minimum(k0, M - k0).astype(F32)
    base = q0 * q0 + wave * wave
    gain = sigma * wave * F32(2.0 / (math.sqrt(math.pi) * M))
    for v in range(4):
        k1 = 16 * me + 4 * v + lane // 32
        q1 = k1.astype(F32)
        value = gain / (base + q1 * q1)
        if v == 0:
            alone = k1 == 0
            value = jnp.where(alone, 0.5 * value, value)
            top = jnp.where(alone, 0.5 * gain / (base + F32(N) * F32(N)), value)
            amp[4] = top
        else:
            amp[4 + v] = value
        amp[v] = value


def columns(first, last, got, amp, col_forward, col_back, col_turn, mid_forward, mid_back, out):
    tiles = list(range(2 * first, 2 * last))
    pieces = jnp.concatenate([got[pl.ds(t, 128, stride=8), :] for t in tiles], axis=1)
    spec = product((col_forward[0], col_forward[1]), split(pieces), NN)
    parts = []
    for i in range(len(tiles)):
        lanes = slice(128 * i, 128 * i + 128)
        re, im = spec[:KS, lanes], spec[KS:, lanes]
        cos, sin = col_turn[0], col_turn[1]
        parts.append(jnp.concatenate([re * cos + im * sin, im * cos - re * sin], axis=1))
    full = product(split(jnp.concatenate(parts, axis=0)), (mid_forward[0], mid_forward[1]), NN)
    factor = jnp.concatenate([amp[t] for t in tiles], axis=0)
    full = full * jnp.concatenate([factor, factor], axis=1)
    back = product(split(full), (mid_back[0], mid_back[1]), NN)
    sides = []
    for i in range(len(tiles)):
        rows = slice(KS * i, KS * i + KS)
        re, im = back[rows, :128], back[rows, 128:]
        cos, sin = col_turn[2], col_turn[3]
        sides.append(jnp.concatenate([re * cos - im * sin, im * cos + re * sin], axis=0))
    high, low = split(jnp.concatenate(sides, axis=1))
    field = lax.dot_general(col_back[...], jnp.concatenate([high, low, high], axis=0), NN, preferred_element_type=F32)
    lane = lax.broadcasted_iota(jnp.int32, (64, 128), 1)
    for i, t in enumerate(tiles):
        here = field[:, 128 * i : 128 * i + 128]
        later, sooner = pltpu.roll(here, 32, 1), pltpu.roll(here, 96, 1)
        out[pl.ds(t, 64, stride=16), :] = jnp.where(lane < 32, pltpu.roll(later, 1, 0), later)
        out[pl.ds(8 + t, 64, stride=16), :] = jnp.where(lane >= 96, pltpu.roll(sooner, 63, 0), sooner)


def rows_back(got, row_back, row_turn, arrive, put):
    arrive(0)
    blocks = [got[pl.ds(t, 128, stride=8), :].T for t in range(4)]
    re = split(jnp.concatenate(blocks, axis=0))
    arrive(1)
    blocks += [got[pl.ds(t, 128, stride=8), :].T for t in range(4, 8)]
    row = lax.broadcasted_iota(jnp.int32, (128, 128), 0)
    lane = lax.broadcasted_iota(jnp.int32, (128, 128), 1)
    sign = (1 - 2 * (lane[:8] % 2)).astype(F32)
    tops = [jnp.broadcast_to(blocks[4][32 * g : 32 * g + 8, :1], (8, 128)) * sign for g in range(4)]
    blocks[4] = jnp.where((row % 32 < 8) & (lane == 0), 0.0, blocks[4])
    im = split(jnp.concatenate(blocks[4:], axis=0))
    sides = [jnp.concatenate(pair, axis=1) for pair in zip(re, im)]
    q = product(sides, (row_back[0], row_back[1]), NN)
    for h in range(2):
        for g in range(4):
            zs = []
            for kv in range(16):
                at = 128 * (kv // 4) + 32 * g + 8 * (kv % 4)
                rows = slice(at, at + 8)
                zr, zi = q[rows, 128 * h : 128 * h + 128], q[rows, 256 + 128 * h : 384 + 128 * h]
                cos = row_turn[0, kv : kv + 1, 128 * h : 128 * h + 128]
                sin = row_turn[1, kv : kv + 1, 128 * h : 128 * h + 128]
                zs.append((zr, zi) if kv == 0 else (zr * cos - zi * sin, zi * cos + zr * sin))
            for a, value in enumerate(back_dft_real_first_half(zs)):
                put(8 * g, 256 * a + 128 * h, value + tops[g])


def gather_observations(me, cells, values, counts, means, hot, parts):
    counts[...] = jnp.zeros_like(counts)

    @pl.loop(0, 8)
    def _(c):
        for i in range(8):
            cell = cells[pl.ds(8 * c + i, 1), :]
            value = values[pl.ds(8 * c + i, 1), :]
            row = cell // N - FIELD * me
            col = cell % N
            inside = (row >= 0) & (row < FIELD)
            spot = jnp.where(inside, (row // 8) * 128 + (col // 128) * 8 + row % 8, -1)
            lane = jnp.where(inside, col % 128, -1)
            lanes = slice(128 * i, 128 * i + 128)
            here = lax.broadcasted_iota(jnp.int32, (256, 128), 0) == spot
            hot[c, :, lanes] = jnp.where(here, 1.0, 0.0).astype(BF16)
            there = lax.broadcasted_iota(jnp.int32, (128, 128), 0) == lane
            high = value.astype(BF16).astype(F32)
            middle = (value - high).astype(BF16).astype(F32)
            low = value - high - middle
            for j, piece in enumerate((jnp.ones_like(value), high, middle, low)):
                parts[128 * j : 128 * j + 128, lanes] = jnp.where(there, piece, 0.0).astype(BF16)
        counts[...] += lax.dot_general(hot[c], parts[...], NT, preferred_element_type=F32)

    number = counts[:, :128]
    total = counts[:, 128:256] + counts[:, 256:384] + counts[:, 384:]
    means[...] = total / jnp.maximum(number, 1.0)


def spread_observations(me, cells, values, means, hot, spread):
    turned_means = jnp.concatenate([means[:128, :].T, means[128:, :].T], axis=1)
    pieces = jnp.concatenate(split(turned_means), axis=0)
    spread[...] = jnp.zeros_like(spread)

    @pl.loop(0, 8)
    def _(c):
        totals = [jnp.zeros((8, 128), F32) for _ in range(4)]
        for b in range(4):
            picked = jnp.dot(pieces, hot[c, :, 256 * b : 256 * b + 256], preferred_element_type=F32)
            for i in range(2):
                cell = cells[pl.ds(8 * c + 2 * b + i, 1), :]
                value = values[pl.ds(8 * c + 2 * b + i, 1), :]
                row = cell // N - FIELD * me
                lane = jnp.where((row >= 0) & (row < FIELD), cell % 128, -1)
                lanes = slice(128 * i, 128 * i + 128)
                mean = picked[:128, lanes] + picked[128:, lanes]
                there = lax.broadcasted_iota(jnp.int32, (128, 128), 0) == lane
                off = jnp.where(there, value - mean, 0.0)
                off = off * off
                for k in range(16):
                    totals[k % 4] = totals[k % 4] + off[8 * k : 8 * k + 8]
        spread[...] += (totals[0] + totals[1]) + (totals[2] + totals[3])


def exchange_edges(me, own_low, own_high, ext, sems):
    up, down = lax.rem(me + 1, DEVICES), lax.rem(me + DEVICES - 1, DEVICES)
    return [
        pltpu.make_async_remote_copy(
            src_ref=own_low, dst_ref=ext.at[pl.ds(24, 8), :], send_sem=sems.at[0], recv_sem=sems.at[1],
            device_id=(down,), device_id_type=MESH,
        ),
        pltpu.make_async_remote_copy(
            src_ref=own_high, dst_ref=ext.at[pl.ds(0, 8), :], send_sem=sems.at[2], recv_sem=sems.at[3],
            device_id=(up,), device_id_type=MESH,
        ),
    ]


TILES = N // 128
OWN = slice(8, 24)


def tile(j):
    return slice(128 * j, 128 * j + 128)


def neighbours(load):
    lane = lax.broadcasted_iota(jnp.int32, (32, 128), 1)
    values = [load(0), load(1)]
    rights = [pltpu.roll(v, 1, 1) for v in values]
    lefts = [pltpu.roll(v, 127, 1) for v in values]
    before = jnp.zeros_like(rights[0])
    for j in range(TILES):
        if j == TILES - 1:
            after = jnp.zeros_like(before)
        else:
            after = lefts[1]
        west = jnp.where(lane == 0, before, rights[0])
        east = jnp.where(lane == 127, after, lefts[0])
        north = pltpu.roll(values[0], 1, 0)
        south = pltpu.roll(values[0], 31, 0)
        yield j, values[0], north, south, west, east
        before = rights[0]
        if j + 1 < TILES:
            values = values[1:]
            rights = rights[1:]
            lefts = lefts[1:]
            if j + 2 < TILES:
                values.append(load(j + 2))
                rights.append(pltpu.roll(values[1], 1, 1))
                lefts.append(pltpu.roll(values[1], 127, 1))


def krylov(me, lx, sx, kappa, coefs, diag, v0, z0, z1, z2):
    row = lax.broadcasted_iota(jnp.int32, (32, 128), 0)
    lane = lax.broadcasted_iota(jnp.int32, (32, 128), 1)
    valid = ((row >= 8) | (me > 0)) & ((row < 24) | (me < DEVICES - 1))
    for j in range(TILES):
        kappa[:, tile(j)] = jnp.where(valid, jnp.exp(lx[:, tile(j)]), 0.0)
    sums = [jnp.zeros((16, 128), F32) for _ in range(8)]
    for j, k, kn, ks, kw, ke in neighbours(lambda j: kappa[:, tile(j)]):
        north, south, west, east = 0.5 * (k + kn), 0.5 * (k + ks), 0.5 * (k + kw), 0.5 * (k + ke)
        d = north + south + west + east
        inverse = jnp.where(valid, 1.0 / d, 0.0)
        coefs[0, :, tile(j)] = north * inverse
        coefs[1, :, tile(j)] = south * inverse
        coefs[2, :, tile(j)] = west * inverse
        coefs[3, :, tile(j)] = east * inverse
        source = sx[:, tile(j)]
        first = source * inverse
        diag[:, tile(j)] = d[OWN]
        v0[:, tile(j)] = first
        sums[0] = sums[0] + source[OWN] * first[OWN]

    def beside(values):
        for j, v, vn, vs, vw, ve in neighbours(lambda j: values[:, tile(j)]):
            yield j, v, (coefs[0, :, tile(j)] * vn + coefs[1, :, tile(j)] * vs) + (
                coefs[2, :, tile(j)] * vw + coefs[3, :, tile(j)] * ve
            )

    for j, v, s in beside(v0):
        z = v - s
        z0[:, tile(j)] = z
        own = z[OWN]
        sums[1] = sums[1] + sx[OWN, tile(j)] * own
        sums[2] = sums[2] + diag[:, tile(j)] * own * own
    for j, v, s in beside(z0):
        z = -s
        z1[:, tile(j)] = z
        own = diag[:, tile(j)] * z[OWN]
        sums[3] = sums[3] + own * v[OWN]
        sums[4] = sums[4] + own * z[OWN]
    for j, v, s in beside(z1):
        z = -2.0 * s - z0[:, tile(j)]
        z2[:, tile(j)] = z
        own = diag[:, tile(j)] * z[OWN]
        sums[5] = sums[5] + own * v[OWN]
        sums[6] = sums[6] + own * z[OWN]
    for j, v, s in beside(z2):
        z = -2.0 * s[OWN] - z1[OWN, tile(j)]
        sums[7] = sums[7] + diag[:, tile(j)] * v[OWN] * z
    return sums


def lane_totals(sums):
    count = len(sums)
    high = -(-count // 8) * 8
    rows = [jnp.sum(s, axis=0, keepdims=True) for s in sums] + [jnp.zeros((1, 128), F32)] * (high - count)
    rows = jnp.concatenate(rows, axis=0)
    totals = jnp.broadcast_to(jnp.sum(rows, axis=1, keepdims=True), (high, 128))
    at = lax.broadcasted_iota(jnp.int32, (high, 128), 0) == lax.broadcasted_iota(jnp.int32, (high, 128), 1)
    return jnp.sum(jnp.where(at, totals, 0.0), axis=0, keepdims=True)


def share(me, row, mine, all_rows, sems):
    mine[0:1, :] = row
    all_rows[pl.ds(me, 1), :] = row
    send_to_all(me, others_far_first, lambda d: mine.at[pl.ds(0, 1), :], lambda s: all_rows.at[pl.ds(s, 1), :], sems.at[0], sems.at[1])


def shared(me, all_rows, sems):
    wait_for_all(me, all_rows.at[pl.ds(0, DEVICES - 1), :], sems.at[0], sems.at[1])


PAIRS = [(i, j) for i in range(4) for j in range(i, 4)]


def misfit_parts(guess, fields, counts, means, spread):
    sums = [spread[...]] + [jnp.zeros((8, 128), F32) for _ in range(14)]
    for j in range(TILES):
        for g in range(2):
            rows = slice(128 * g + 8 * j, 128 * g + 8 * j + 8)
            us = [f[8 + 8 * g : 16 + 8 * g, tile(j)] for f in fields]
            n = counts[rows, :128]
            off = ((guess[0] * us[0] + guess[1] * us[1]) + (guess[2] * us[2] + guess[3] * us[3])) - means[rows, :]
            many = n * off
            sums[0] = sums[0] + many * off
            for i in range(4):
                sums[1 + i] = sums[1 + i] + many * us[i]
            scaled_us = [n * u for u in us]
            for k, (i, l) in enumerate(PAIRS):
                sums[5 + k] = sums[5 + k] + scaled_us[i] * us[l]
    row = lane_totals(sums)
    lane = lax.broadcasted_iota(jnp.int32, (1, 128), 1)
    for i in range(4):
        row = jnp.where(lane == 15 + i, guess[i][:1], row)
    return pltpu.roll(jnp.broadcast_to(row, (8, 128)), 8, 1)[:1]


def misfit(y, rows):
    table = rows.T[8:]
    off = [y[i][:1] - table[15 + i : 16 + i] for i in range(4)]
    total = table[0:1]
    for i in range(4):
        total = total + 2.0 * off[i] * table[1 + i : 2 + i]
    for k, (i, l) in enumerate(PAIRS):
        term = off[i] * off[l] * table[5 + k : 6 + k]
        total = total + (term if i == l else 2.0 * term)
    return jnp.sum(total)


def pair_sum(x, y):
    total = x[0] + y[0]
    step = total - x[0]
    rest = (x[0] - (total - step)) + (y[0] - step)
    rest = rest + (x[1] + y[1])
    high = total + rest
    return high, rest - (high - total)


def pair_scaled(x, factor):
    return x[0] * F32(factor), x[1] * F32(factor)


def pair_total(rows):
    zero = jnp.zeros((8, 128), F32)
    terms = [(rows[8 * k : 8 * k + 8], zero) for k in range(DEVICES // 8)]
    while len(terms) > 1:
        terms = [pair_sum(terms[2 * k], terms[2 * k + 1]) for k in range(len(terms) // 2)]
    total = terms[0]
    for shift in (4, 2, 1):
        total = pair_sum(total, (pltpu.roll(total[0], shift, 0), pltpu.roll(total[1], shift, 0)))
    return total


def cut(a):
    t = F32(4097.0) * a
    high = t - (t - a)
    return high, a - high


def system(take, scale, add):
    g0, e0, m0, m1, q11, q12, q22, q23 = take

    def less(a, b):
        return add(a, scale(b, -1.0))

    m = [m0, m1, less(scale(q11, 2.0), m0), less(scale(q12, 2.0), m1), less(scale(q22, 2.0), m0), less(scale(q23, 2.0), m1)]

    def inner(i, j):
        return scale(add(m[i + j], m[abs(i - j)]), 0.5)

    def energy(i, j):
        return add(inner(i, j), scale(add(inner(i, j + 1), inner(i, abs(j - 1))), 0.5))

    gram = [[None] * 4 for _ in range(4)]
    gram[0][0] = e0
    for j in range(3):
        gram[j + 1][0] = inner(0, j)
        for i in range(j + 1):
            gram[j + 1][i + 1] = energy(i, j)
    tail = less(m0, e0)
    return gram, [g0, e0, tail, less(scale(less(m1, tail), 2.0), e0)]


def lanes_of(row):
    return [jnp.broadcast_to(row[:1, i : i + 1], (8, 128)) for i in range(8)]


def solver(gram):
    gram = [list(r) for r in gram]
    factors = [[None] * 4 for _ in range(4)]
    inverse = []
    whole = [gram[i][i] for i in range(4)]
    for k in range(4):
        pivot = gram[k][k]
        inverse.append(jnp.where(pivot > 1e-6 * whole[k], 1.0 / pivot, 0.0))
        for i in range(k + 1, 4):
            factors[i][k] = gram[i][k] * inverse[k]
        for i in range(k + 1, 4):
            for j in range(k + 1, i + 1):
                gram[i][j] = gram[i][j] - factors[i][k] * gram[j][k]

    def solve(right):
        right = list(right)
        for k in range(4):
            for i in range(k + 1, 4):
                right[i] = right[i] - factors[i][k] * right[k]
        out = [right[k] * inverse[k] for k in range(4)]
        for k in (2, 1, 0):
            for i in range(k + 1, 4):
                out[k] = out[k] - factors[i][k] * out[i]
        return out

    return solve


def weights(row):
    gram, right = system(lanes_of(row), lambda a, f: a * F32(f), lambda a, b: a + b)
    return solver(gram)(right)


def refined_weights(total):
    gram, right = system(list(zip(lanes_of(total[0]), lanes_of(total[1]))), pair_scaled, pair_sum)
    solve = solver([[g and g[0] for g in r] for r in gram])
    y = solve([r[0] for r in right])
    y_cut = [cut(v) for v in y]
    cuts = [[g and cut(g[0]) for g in r] for r in gram]
    left = []
    for i in range(4):
        rest = right[i]
        for j in range(4):
            a, b = max(i, j), min(i, j)
            high, low = gram[a][b]
            (gh, gl), (yh, yl) = cuts[a][b], y_cut[j]
            main = high * y[j]
            error = ((gh * yh - main) + (gh * yl + gl * yh)) + gl * yl
            rest = pair_sum(rest, (-main, -(error + low * y[j])))
        left.append(rest[0] + rest[1])
    better = [v + d for v, d in zip(y, solve(left))]
    size = jnp.maximum(jnp.maximum(jnp.abs(y[0]), jnp.abs(y[1])), jnp.maximum(jnp.abs(y[2]), jnp.abs(y[3])))
    close = jnp.abs(better[0] - y[0]) <= 0.01 * size
    for k in range(1, 4):
        close = close & (jnp.abs(better[k] - y[k]) <= 0.01 * size)
    return [jnp.where(close, b, v) for b, v in zip(better, y)]


LOADS = ("state", "noise", "source", "cells", "values",
         "row_forward", "row_back", "row_turn", "col_forward", "col_back", "col_turn", "mid_forward", "mid_back")


def kernel(*refs):
    (step, sigma, wave), refs = refs[:3], refs[3:]
    count = len(LOADS)
    sources, refs = refs[:count], refs[count:]
    (log_perm_out, pressure_out, loglik), refs = refs[:3], refs[3:]
    held, refs = refs[:count], refs[count:]
    (
        z_high, z_low, sent1, got1, amp, sent2, got2,
        counts, means, hot, parts, spread,
        lx, sx, kappa, coefs, diag, v0, z0, z1, z2, mine, everyone, pressure, sems, load_sems, edge_sems, end_sems,
    ) = refs
    me = lax.axis_index(AXIS)
    loads = {
        name: pltpu.make_async_copy(sources[k], held[k], load_sems.at[k]) for k, name in enumerate(LOADS)
    }
    early = ("state", "noise", "row_turn", "row_forward")
    for name in early:
        loads[name].start()
    (state, noise, source, cells, values,
     row_forward, row_back, row_turn, col_forward, col_back, col_turn, mid_forward, mid_back) = held
    greet_all(me)
    for name in early:
        loads[name].wait()
    for name in LOADS:
        if name not in early:
            loads[name].start()
    rows_forward(step[0], state, noise, row_turn, z_high, z_low, row_forward, sent1)
    loads["source"].wait()
    meet_all()
    for part, (first, last) in enumerate(ARRIVALS):
        size = 2 * (last - first)
        send_to_all(
            me, others_far_first, lambda d: sent1.at[pl.ds(8 * d + 2 * first, size), :],
            lambda s: got1.at[pl.ds(8 * s + 2 * first, size), :], sems.at[2 * part], sems.at[2 * part + 1],
        )
    source_edges = exchange_edges(me, source.at[pl.ds(0, 8), :], source.at[pl.ds(8, 8), :], sx, edge_sems)
    for copy in source_edges:
        copy.start()
    own = pl.ds(pl.multiple_of(8 * me, 8), 8)
    got1[own, :] = sent1[own, :]
    sx[OWN, :] = source[...]
    amplitudes(me, sigma[0], wave[0], amp)
    for name in ("col_forward", "col_back", "col_turn", "mid_forward", "mid_back", "row_back", "cells", "values"):
        loads[name].wait()
    gather_observations(me, cells, values, counts, means, hot, parts)
    ready = 0
    for part, (first, last) in enumerate(DEPARTURES):
        while ready < len(ARRIVALS) and ARRIVALS[ready][0] < last:
            size = 2 * (ARRIVALS[ready][1] - ARRIVALS[ready][0])
            wait_for_all(me, got1.at[pl.ds(0, size * (DEVICES - 1)), :], sems.at[2 * ready], sems.at[2 * ready + 1])
            ready += 1
        columns(first, last, got1, amp, col_forward, col_back, col_turn, mid_forward, mid_back, sent2)
        size = 2 * (last - first)
        send_to_all(
            me, others_far_first, lambda d: sent2.at[pl.ds(8 * d + 2 * first, size), :],
            lambda s: got2.at[pl.ds(8 * s + 2 * first, size), :], sems.at[8 + 2 * part], sems.at[9 + 2 * part],
        )
    got2[own, :] = sent2[own, :]
    spread_observations(me, cells, values, means, hot, spread)
    def arrive(part):
        size = 2 * (DEPARTURES[part][1] - DEPARTURES[part][0])
        wait_for_all(me, got2.at[pl.ds(0, size * (DEVICES - 1)), :], sems.at[8 + 2 * part], sems.at[9 + 2 * part])

    def put(row, at, value):
        lx[row : row + 8, at : at + 128] = value

    rows_back(got2, row_back, row_turn, arrive, put)
    write = pltpu.make_async_copy(lx.at[pl.ds(8, FIELD), :], log_perm_out, load_sems.at[count])
    write.start()
    for copy in source_edges:
        copy.wait()
    sums = krylov(me, lx, sx, kappa, coefs, diag, v0, z0, z1, z2)
    row = lane_totals(sums)
    fields = (v0, z0, z1, z2)
    guess = weights(row)
    fine = jnp.abs(guess[0]) < 64.0
    for i in range(1, 4):
        fine = fine & (jnp.abs(guess[i]) < 64.0)
    guess = [jnp.where(fine, g, 0.0) for g in guess]
    share(me, row + misfit_parts(guess, fields, counts, means, spread), mine, everyone, end_sems)
    shared(me, everyone, end_sems)
    y = refined_weights(pair_total(everyone[...]))
    for j in range(TILES):
        for g in range(2):
            us = [f[8 + 8 * g : 16 + 8 * g, tile(j)] for f in fields]
            pressure[8 * g : 8 * g + 8, tile(j)] = (y[0] * us[0] + y[1] * us[1]) + (y[2] * us[2] + y[3] * us[3])
    write_pressure = pltpu.make_async_copy(pressure, pressure_out, load_sems.at[count + 1])
    write_pressure.start()
    loglik[0, 0] = F32(-2.0 / 8192) * misfit(y, everyone[...])
    write.wait()
    write_pressure.wait()


def finish(log_perm, pressure, loglik, log_perm_out, pressure_out, loglik_out, sems):
    copies = [
        pltpu.make_async_copy(log_perm, log_perm_out, sems.at[0]),
        pltpu.make_async_copy(pressure, pressure_out, sems.at[1]),
    ]
    for copy in copies:
        copy.start()
    loglik_out[0, 0] = loglik[0, 0]
    for copy in copies:
        copy.wait()


def body(state, noise, step, field_scale, wave_scale, source, obs_cells, obs_values):
    anywhere = pl.BlockSpec(memory_space=pl.ANY)
    smem = pl.BlockSpec(memory_space=pltpu.SMEM)
    field = pltpu.VMEM((32, N), F32)
    own = pltpu.VMEM((FIELD, N), F32)
    arrays = [state, noise, source, obs_cells.reshape(64, 128), obs_values.reshape(64, 128)]
    arrays += [jnp.asarray(t) for t in tables()]
    log_perm, pressure, loglik = pl.pallas_call(
        kernel,
        out_shape=(
            jax.ShapeDtypeStruct((FIELD, N), F32),
            jax.ShapeDtypeStruct((FIELD, N), F32),
            jax.ShapeDtypeStruct((1, 1), F32),
        ),
        in_specs=[pl.BlockSpec(memory_space=pltpu.SMEM)] * 3 + [anywhere] * len(arrays),
        out_specs=(anywhere, anywhere, smem),
        scratch_shapes=[
            pltpu.VMEM(a.shape, a.dtype) for a in arrays
        ] + [
            pltpu.VMEM((512, 512), BF16),
            pltpu.VMEM((512, 512), BF16),
            pltpu.VMEM((1024, 128), F32),
            pltpu.VMEM((1024, 128), F32),
            pltpu.VMEM((8, KS, 128), F32),
            pltpu.VMEM((1024, 128), F32),
            pltpu.VMEM((1024, 128), F32),
            pltpu.VMEM((256, 512), F32),
            pltpu.VMEM((256, 128), F32),
            pltpu.VMEM((8, 256, 1024), BF16),
            pltpu.VMEM((512, 1024), BF16),
            pltpu.VMEM((8, 128), F32),
            field,
            field,
            field,
            pltpu.VMEM((4, 32, N), F32),
            own,
            field,
            field,
            field,
            field,
            pltpu.VMEM((8, 128), F32),
            pltpu.VMEM((DEVICES, 128), F32),
            own,
            pltpu.SemaphoreType.DMA((16,)),
            pltpu.SemaphoreType.DMA((len(arrays) + 2,)),
            pltpu.SemaphoreType.DMA((4,)),
            pltpu.SemaphoreType.DMA((2,)),
        ],
        compiler_params=pltpu.CompilerParams(collective_id=0, has_side_effects=True, vmem_limit_bytes=40 * 2**20),
    )(step, field_scale, wave_scale, *[pltpu.with_memory_space_constraint(a, pltpu.HBM) for a in arrays])
    log_perm, pressure, loglik = pl.pallas_call(
        finish,
        out_shape=(
            jax.ShapeDtypeStruct((FIELD, N), F32),
            jax.ShapeDtypeStruct((FIELD, N), F32),
            jax.ShapeDtypeStruct((1, 1), F32),
        ),
        in_specs=[anywhere, anywhere, smem],
        out_specs=(anywhere, anywhere, smem),
        scratch_shapes=[pltpu.SemaphoreType.DMA((2,))],
        compiler_params=pltpu.CompilerParams(vmem_limit_bytes=2**20),
    )(log_perm, pressure, loglik)
    return log_perm, pressure, loglik.reshape(())


def solution(mesh):
    in_specs = (P(AXIS, None), P(AXIS, None), P(), P(), P(), P(AXIS, None), P(), P())
    out_specs = (P(AXIS, None), P(AXIS, None), P())
    return jax.shard_map(body, mesh=mesh, in_specs=in_specs, out_specs=out_specs, check_vma=False)
```
